512 devices in a mesh: seq: 32 (over x, y, core), exp: 16 (over z).
Axes of the slice: x: 4, y: 4, z: 16, core: 2. Of those that a mesh axis runs over, the one named last changes fastest.
Arguments:
- hidden_in: bfloat16 [16, 4096, 2048], P('exp', 'seq'), may hold values from -6 to 6
- route_ids: int32 [16, 4096, 2], P('exp', 'seq'), may hold values from 0 to 15, all different within a row; in each aligned block of 128 rows (0 to 127, 128 to 255, ..., all dimensions but the last counted through in order) at most 32 rows name the same one
- route_gates: float32 [16, 4096, 2], P('exp', 'seq'), may hold values from 0.1 to 1
- language: int32 [16, 4096], P('exp', 'seq'), may hold values from 0 to 7
- allowed: int32 [8, 8], replicated, may hold values from 0 to 15, all different within a row
- w_gate: bfloat16 [16, 2048, 512], P('exp', 'seq'), may hold values from -0.125 to 0.125
- w_up: bfloat16 [16, 2048, 512], P('exp', 'seq'), may hold values from -0.125 to 0.125
- w_down: bfloat16 [16, 512, 2048], P('exp', 'seq'), may hold values from -0.25 to 0.25
- gate_proj: bfloat16 [2048, 64], replicated, may hold values from -0.125 to 0.125
- head_decay: float32 [32], replicated, may hold values from -13 to -2
- query_in: bfloat16 [16, 4096, 2048], P('exp', 'seq'), may hold values from -6 to 6
- key_in: bfloat16 [16, 4096, 2048], P('exp', 'seq'), may hold values from -6 to 6
- value_in: bfloat16 [16, 4096, 4096], P('exp', 'seq'), may hold values from -6 to 6
- block_inverse: bfloat16 [16, 4096, 2048], P('exp', 'seq'), may hold values from -0.29882812 to 0.29882812
Outputs:
- routed: bfloat16 [16, 4096, 2048], P('exp', 'seq')
- core_out: bfloat16 [16, 4096, 4096], P('exp', 'seq')
The draws below stay inside these ranges and needn't reach their ends.
Inputs may be any that keep to these rules, and one draw needn't show every extreme that they name: `route_ids`: among the routes of the rows of one device, no expert is named more than 32 times, a bound that some block reaches. `allowed`: each of its rows names 8 different experts, and every expert is allowed for some language.
All inputs are finite; a program needn't handle non-finite values.
Results may differ from the reference program's by a relative error of at most 0.019.
Values may be sent and summed in bfloat16 or wider, within the bound.
A program may use at most 64 MiB of HBM per device.

```python
import math
import jax
import jax.numpy as jnp
import numpy as np
from jax import lax

D = 2048
FF_E = 512
HK = 16
HV = 32
DK = 128
DV = 128
TOK_DEV = 128
BLOCK_LEN = 64
TOPW = 2
LANGS = 8
EXPERTS = 16
ALLOW = 8
CAP = 32
SEQS = 16
LEN = 4096


def draw_head_decay(key, part):
    key_slow, key_level = jax.random.split(jax.random.fold_in(key, 11))
    share = 0.5
    slow = jax.random.uniform(key_slow, (HV,), jnp.float32) < share
    level = jax.random.uniform(key_level, (HV,), jnp.float32)
    slow_rate = jnp.log(0.1 / LEN) + level * jnp.log(15.0)
    fast_rate = jnp.log(0.03) + level * jnp.log(3.0)
    return jnp.where(slow, slow_rate, fast_rate).astype(jnp.float32)


def with_ends(entries, own_key, smallest, largest):
    longest = entries.shape.index(max(entries.shape))
    spots = []
    for shift in (0, 1):
        where = [jax.random.randint(jax.random.fold_in(own_key, axis), (), 0, length) for axis, length in enumerate(entries.shape)]
        where[longest] = (where[longest] + shift) % entries.shape[longest]
        spots.append(tuple(where))
    return entries.at[spots[0]].set(smallest).at[spots[1]].set(largest)


def block_levels(key, extent, pieces, smallest, high):
    def one(axis_at, parts):
        draws = jax.random.uniform(jax.random.fold_in(jax.random.fold_in(key, 6), axis_at), (parts,), jnp.float32, smallest / len(pieces), high / len(pieces))
        return jnp.repeat(jnp.exp(draws), extent[axis_at] // parts).reshape((-1,) + (1,) * (len(extent) - axis_at - 1))

    gain = one(*pieces[0])
    for cut in pieces[1:]:
        gain = gain * one(*cut)
    return gain


def rank_bounds(number_of, lean):
    portions = [(1 << 20) // math.isqrt(rank ** lean) + 1 for rank in range(1, number_of + 1)]
    width = 1 + sum(portions) // (1 << 30)
    return np.cumsum(np.array([max(1, weight // width) for weight in portions]))


def ranked(stream_key, shape, amount, slope):
    grid = rank_bounds(amount, slope)
    ticket = jax.random.randint(jax.random.fold_in(stream_key, 1), shape, 0, int(grid[amount - 1]))
    grade = jnp.searchsorted(jnp.asarray(grid, jnp.int32), ticket, side="right")
    return jax.random.permutation(jax.random.fold_in(stream_key, 2), amount)[grade].astype(jnp.int32)


def choose_distinct(rng, rows, number_of, top, lift):
    ranking = jax.random.permutation(jax.random.fold_in(rng, 1), number_of)
    pull = ranking
    for power in range(3):
        pull = pull * pull // number_of
    pull = pull * lift // number_of
    lots = jax.random.randint(jax.random.fold_in(rng, 2), (rows, number_of), 0, 4096) + pull
    sure = jax.random.permutation(jax.random.fold_in(rng, 3), rows)[jnp.arange(number_of) % rows]
    lots = jnp.where(jnp.arange(rows)[:, None] == sure[None, :], 1 << 14, lots)
    merit = lots * number_of + jnp.arange(number_of)
    return lax.top_k(merit.astype(jnp.int32), top)[1].astype(jnp.int32)


def shared_out(rng, own, number, rows, number_of, top, reach, skew):
    sequence = jax.random.permutation(rng, number_of)
    crowded, common = portions_of(number_of, rows * top, reach, skew, True), portions_of(number_of, rows * top, reach, skew, False)
    places = jnp.arange(number_of)

    def named(lengths, turn):
        used = int((lengths > 0).sum())
        fixed = max(1, used // 4)
        shifted = fixed + (places - fixed + turn * (used - fixed)) % max(1, number_of - fixed)
        return jnp.zeros((number_of,), jnp.int32).at[sequence[jnp.where(places < fixed, places, shifted)]].set(jnp.asarray(lengths, jnp.int32))

    lengths = jnp.where(number % 4 == 0, named(crowded, number // 4), named(common, number - number // 4 - 1))
    mixed = jax.random.permutation(jax.random.fold_in(own, 3), number_of)
    source_of, sink = mixed[0:number_of // 2 * 2:2], mixed[1:number_of // 2 * 2:2]
    room = jnp.minimum(lengths[source_of] - 1, reach - lengths[sink]) // 2
    room = jnp.where((source_of == sequence[0]) | (sink == sequence[0]) | (lengths[sink] == 0), 0, jnp.maximum(room, 0))
    shifted = jax.random.randint(jax.random.fold_in(own, 4), (number_of // 2,), 0, 1 << 20) % (room + 1)
    lengths = lengths.at[source_of].add(-shifted).at[sink].add(shifted)
    items = jnp.searchsorted(jnp.cumsum(lengths), jnp.arange(rows * top), side="right").astype(jnp.int32)
    listing = items.reshape(top, rows).T
    listing = listing[jax.random.permutation(jax.random.fold_in(own, 1), rows)]
    turn = jax.random.randint(jax.random.fold_in(own, 2), (rows, 1), 0, top)
    return jnp.take_along_axis(listing, (jnp.arange(top)[None, :] + turn) % top, axis=1)


def portions_of(count, total, reach, lean, full):
    portions = [(1 << 20) // math.isqrt(grade ** lean) + 1 for grade in range(1, count + 1)]
    largest = reach if full else min(reach, max(-(-total // count), total * portions[0] // sum(portions)))
    least = 1 if total - largest >= count - 1 else 0
    holding, rest = [largest] + [least] * (count - 1), total - largest - least * (count - 1)
    while rest > 0:
        movable = [i for i in range(1, count) if holding[i] < largest] or [i for i in range(1, count) if holding[i] < reach]
        pool, left = sum([portions[i] for i in movable]), rest
        for i in movable:
            more = min(reach - holding[i], max(1, left * portions[i] // pool), rest)
            holding[i] = holding[i] + more
            rest = rest - more
    return np.array(holding)


def bell_draw(stream_key, shape, deviation, bound, shards=(), kind=jnp.bfloat16):
    factor_of = block_levels(stream_key, shape, shards, -0.22, 0.18) if shards else 1.0
    drawn = jax.random.normal(stream_key, shape, jnp.float32) * deviation * factor_of
    return jnp.minimum(jnp.maximum(drawn, -bound), bound).astype(kind)


def setup_inputs(seed: int = 0) -> dict:
    seeds = jax.random.split(jax.random.key(seed), 15)
    hidden_in = bell_draw(seeds[0], (SEQS, LEN, D), 1.0, 6.0, ((0, 16), (1, 32)))
    route_ids_keys = jax.random.split(jax.random.fold_in(seeds[1], 1), SEQS * LEN // TOK_DEV)
    route_ids_turns = jax.random.permutation(jax.random.fold_in(seeds[1], 3), SEQS * LEN // TOK_DEV)
    route_ids = jax.vmap(lambda own, number: shared_out(jax.random.fold_in(seeds[1], 2), own, number, TOK_DEV, EXPERTS, TOPW, CAP, 2))(route_ids_keys, route_ids_turns).reshape((SEQS, LEN, TOPW))
    route_gates = jnp.clip(0.1 + 0.9 * jax.random.uniform(seeds[2], (SEQS, LEN, TOPW), jnp.float32) ** block_levels(seeds[2], (SEQS, LEN, TOPW), ((0, 16), (1, 32)), -0.2, 0.2), 0.1, 1.0)
    language = with_ends(ranked(seeds[3], (SEQS, LEN), LANGS, 2), jax.random.fold_in(seeds[3], 3), 0, LANGS - 1).astype(jnp.int32)
    allowed = choose_distinct(seeds[4], LANGS, EXPERTS, ALLOW, 0)
    w_gate = bell_draw(seeds[5], (EXPERTS, D, FF_E), D ** -0.5, 0.125, ((0, 16), (1, 32)))
    w_up = bell_draw(seeds[6], (EXPERTS, D, FF_E), D ** -0.5, 0.125, ((0, 16), (1, 32)))
    w_down = bell_draw(seeds[7], (EXPERTS, FF_E, D), FF_E ** -0.5, 0.25, ((0, 16), (1, 32)))
    gate_proj = bell_draw(seeds[8], (D, 2 * HV), D ** -0.5, 0.125)
    head_decay = draw_head_decay(jax.random.fold_in(seeds[14], 71), 0)
    query_in = bell_draw(seeds[10], (SEQS, LEN, HK * DK), 1.0, 6.0, ((0, 16), (1, 32)))
    key_in = bell_draw(seeds[11], (SEQS, LEN, HK * DK), 1.0, 6.0, ((0, 16), (1, 32)))
    value_in = bell_draw(seeds[12], (SEQS, LEN, HV * DV), 1.0, 6.0, ((0, 16), (1, 32)))
    block_inverse = bell_draw(seeds[13], (SEQS, LEN, HV * BLOCK_LEN), 0.05, 0.29882812, ((0, 16), (1, 32)))
    return dict(hidden_in=hidden_in, route_ids=route_ids, route_gates=route_gates, language=language, allowed=allowed, w_gate=w_gate, w_up=w_up, w_down=w_down, gate_proj=gate_proj, head_decay=head_decay, query_in=query_in, key_in=key_in, value_in=value_in, block_inverse=block_inverse)


highest = lax.Precision.HIGHEST

def normalized(values, head_count, factor_scale):
    flat_vals = values.astype(jnp.float32)
    shaped = flat_vals.reshape(flat_vals.shape[0], head_count, -1)
    factor = lax.rsqrt(lax.optimization_barrier(jnp.sum(shaped * shaped, axis=-1, keepdims=True)) + 1e-06) * factor_scale
    return (shaped * factor).astype(jnp.bfloat16)

def delta_blocks(queries, key_rows, values, inverse, beta_gate, decay_log):
    head_count, block_count, block_size, key_dim = queries.shape
    value_dim = values.shape[-1]
    cumulative = jnp.cumsum(decay_log, axis=-1)
    eye_mat = jnp.eye(block_size, dtype=jnp.float32)
    strict = jnp.tril(jnp.ones((block_size, block_size), jnp.float32), -1)
    causal = jnp.tril(jnp.ones((block_size, block_size), jnp.bool_))
    solver = (eye_mat + strict * inverse.astype(jnp.float32)).astype(jnp.bfloat16)
    beta_vals = (beta_gate[..., None] * values.astype(jnp.float32)).astype(jnp.bfloat16)
    beta_keys = ((beta_gate * jnp.exp(cumulative))[..., None] * key_rows.astype(jnp.float32)).astype(jnp.bfloat16)
    new_base = jnp.einsum('hnij,hnjd->hnid', solver.astype(jnp.float32), beta_vals.astype(jnp.float32), precision=highest)
    key_mix = jnp.einsum('hnij,hnjd->hnid', solver.astype(jnp.float32), beta_keys.astype(jnp.float32), precision=highest)
    query_gate = queries.astype(jnp.float32) * jnp.exp(cumulative)[..., None]
    spread = jnp.where(causal, cumulative[..., :, None] - cumulative[..., None, :], 0.0)
    scores = jnp.einsum('hnid,hnjd->hnij', queries.astype(jnp.float32), key_rows.astype(jnp.float32), precision=highest)
    weights = jnp.where(causal, scores * jnp.exp(spread), 0.0).astype(jnp.bfloat16)
    tail_decay = jnp.exp(cumulative[..., -1:] - cumulative)
    key_decay = (key_rows.astype(jnp.float32) * tail_decay[..., None]).astype(jnp.bfloat16)
    carry_decay = jnp.exp(cumulative[..., -1])

    def advance(carry_state, inputs):
        mix_now, base_now, gate_now, keyd_now, keep_now = inputs
        fresh_vals = (base_now - jnp.einsum('hid,hde->hie', mix_now, carry_state, precision=highest)).astype(jnp.bfloat16)
        early_out = jnp.einsum('hid,hde->hie', gate_now, carry_state, precision=highest)
        carry_state = keep_now[:, None, None] * carry_state + jnp.einsum('hid,hie->hde', keyd_now.astype(jnp.float32), fresh_vals.astype(jnp.float32), precision=highest)
        return (carry_state, (fresh_vals, early_out))
    moved_seq = tuple((jnp.moveaxis(element, 1, 0) for element in (key_mix, new_base, query_gate, key_decay, carry_decay)))
    initial = jnp.zeros((head_count, key_dim, value_dim), jnp.float32)
    _, (fresh_vals, early_out) = lax.scan(advance, initial, moved_seq)
    fresh_vals = jnp.moveaxis(fresh_vals, 0, 1)
    early_out = jnp.moveaxis(early_out, 0, 1)
    local_out = jnp.einsum('hnij,hnjd->hnid', weights.astype(jnp.float32), fresh_vals.astype(jnp.float32), precision=highest)
    return (early_out + local_out).astype(jnp.bfloat16)

def reference(hidden_in, route_ids, route_gates, language, allowed, w_gate, w_up, w_down, gate_proj, head_decay, query_in, key_in, value_in, block_inverse):
    flat_x = hidden_in.reshape(-1, D)
    total_rows = flat_x.shape[0]
    blocks = total_rows // TOK_DEV
    per_block = TOK_DEV * TOPW
    block_routes = route_ids.reshape(blocks, per_block)
    expert_range = jnp.arange(EXPERTS, dtype=jnp.int32)
    onehot = (block_routes[:, :, None] == expert_range[None, None, :]).astype(jnp.int32)
    earlier = jnp.cumsum(onehot, axis=1) - onehot
    slot_index = lax.optimization_barrier(jnp.sum(earlier * onehot, axis=2))
    block_ids = jnp.arange(blocks, dtype=jnp.int32)[:, None]
    target = block_ids * CAP + slot_index
    token_ids = block_ids * TOK_DEV + jnp.arange(per_block, dtype=jnp.int32)[None, :] // TOPW
    lang_table = jnp.any(allowed[:, :, None] == expert_range[None, None, :], axis=1)
    token_lang = language.reshape(-1)[token_ids]
    permitted = lang_table[token_lang, block_routes].astype(jnp.float32)
    route_weight = route_gates.reshape(blocks, per_block) * permitted
    source_row = jnp.full((EXPERTS, blocks * CAP), total_rows, jnp.int32).at[block_routes, target].set(token_ids)
    slot_weight = jnp.zeros((EXPERTS, blocks * CAP), jnp.float32).at[block_routes, target].set(route_weight)
    padded = jnp.concatenate([flat_x, jnp.zeros((1, D), flat_x.dtype)], axis=0)

    def one_expert(accumul, expert):
        rows_in = padded[source_row[expert]]
        gate_proj_h = jnp.dot(rows_in, w_gate[expert], preferred_element_type=jnp.float32)
        up_proj_h = jnp.dot(rows_in, w_up[expert], preferred_element_type=jnp.float32)
        hidden = (jax.nn.silu(gate_proj_h) * up_proj_h).astype(jnp.bfloat16)
        produced = jnp.dot(hidden, w_down[expert], preferred_element_type=jnp.float32).astype(jnp.bfloat16)
        accumul = accumul.at[source_row[expert]].add(slot_weight[expert][:, None] * produced.astype(jnp.float32), mode='drop')
        return (accumul, None)
    mixed, _ = lax.scan(one_expert, jnp.zeros((total_rows, D), jnp.float32), expert_range)
    routed = mixed.astype(jnp.bfloat16)
    residual = (flat_x.astype(jnp.float32) + routed.astype(jnp.float32)).astype(jnp.bfloat16)
    logits = jnp.dot(residual, gate_proj, preferred_element_type=jnp.float32).astype(jnp.bfloat16)
    beta_all = jax.nn.sigmoid(logits[:, :HV].astype(jnp.float32)).reshape(SEQS, LEN, HV)
    decay_all = (-jnp.exp(head_decay)[None, :] * jax.nn.softplus(logits[:, HV:].astype(jnp.float32))).reshape(SEQS, LEN, HV)
    block_count = LEN // BLOCK_LEN

    def arrange(values):
        return values.reshape(block_count, BLOCK_LEN, HV, -1).transpose(2, 0, 1, 3)

    def one_sequence(inputs):
        queries, key_rows, values, inverse, beta_seq, decay_seq = inputs
        query_n = jnp.repeat(normalized(queries, HK, DK ** (-0.5)), HV // HK, axis=1)
        key_n = jnp.repeat(normalized(key_rows, HK, 0.5), HV // HK, axis=1)
        result = delta_blocks(arrange(query_n), arrange(key_n), arrange(values.reshape(LEN, HV, DV)), arrange(inverse.reshape(LEN, HV, BLOCK_LEN)), beta_seq.reshape(block_count, BLOCK_LEN, HV).transpose(2, 0, 1), decay_seq.reshape(block_count, BLOCK_LEN, HV).transpose(2, 0, 1))
        return result.transpose(1, 2, 0, 3).reshape(LEN, HV * DV)
    core_out = lax.map(one_sequence, (query_in, key_in, value_in, block_inverse, beta_all, decay_all))
    return (routed.reshape(SEQS, LEN, D), core_out)
```

```python
import functools

import jax
import jax.numpy as jnp
from jax import lax
from jax.experimental import pallas as pl
from jax.experimental.pallas import tpu as pltpu
from jax.sharding import PartitionSpec as P

highest = lax.Precision.HIGHEST


def delta_kernel(block_size, q_ref, k_ref, v_ref, inv_ref, gate_ref, rate_ref, out_ref, state_ref, beta_ref, cum_ref):
    step = pl.program_id(0)
    chunk_rows, key_dim = q_ref.shape
    per_chunk = chunk_rows // block_size
    rows_i = lax.broadcasted_iota(jnp.int32, (block_size, block_size), 0)
    cols_i = lax.broadcasted_iota(jnp.int32, (block_size, block_size), 1)
    diagonal = rows_i == cols_i
    below = rows_i > cols_i
    causal = rows_i >= cols_i

    @pl.when(step == 0)
    def _():
        state_ref[...] = jnp.zeros_like(state_ref)
        beta_ref[...] = jax.nn.sigmoid(gate_ref[0].astype(jnp.float32))
        raw = gate_ref[1].astype(jnp.float32)
        soft = jnp.maximum(raw, 0.0) + jnp.log1p(jnp.exp(-jnp.abs(raw)))
        log_decay = -jnp.exp(rate_ref[0, 0]) * soft
        upper = (rows_i <= cols_i).astype(jnp.float32)
        cum_ref[...] = jnp.dot(
            log_decay, upper, precision=highest, preferred_element_type=jnp.float32
        )

    def dot(a, b, contract):
        return lax.dot_general(
            a, b, ((contract[:1], contract[1:]), ((), ())), preferred_element_type=jnp.float32
        )

    def column(row):
        return jnp.sum(jnp.where(diagonal, row, 0.0), axis=1, keepdims=True)

    def normal(values, scale):
        vals = values.astype(jnp.float32)
        factor = lax.rsqrt(jnp.sum(vals * vals, axis=1, keepdims=True) + 1e-06) * scale
        return (vals * factor).astype(jnp.bfloat16)

    state = state_ref[...]
    for piece in range(per_chunk):
        span = pl.ds(piece * block_size, block_size)
        block = step * per_chunk + piece
        cum_row = cum_ref[pl.ds(block, 1), :]
        cum_col = column(cum_row)
        beta_col = column(beta_ref[pl.ds(block, 1), :])
        last = cum_row[:, block_size - 1 :]
        grow = jnp.exp(cum_col)
        query_n = normal(q_ref[span, :], key_dim ** (-0.5))
        key_n = normal(k_ref[span, :], 0.5)
        key_f = key_n.astype(jnp.float32)
        solver = jnp.where(
            diagonal, 1.0, jnp.where(below, inv_ref[span, :].astype(jnp.float32), 0.0)
        ).astype(jnp.bfloat16)
        beta_vals = (beta_col * v_ref[span, :].astype(jnp.float32)).astype(jnp.bfloat16)
        beta_keys = ((beta_col * grow) * key_f).astype(jnp.bfloat16)
        new_base = dot(solver, beta_vals, (1, 0))
        key_mix = dot(solver, beta_keys, (1, 0)).astype(jnp.bfloat16)
        query_gate = (query_n.astype(jnp.float32) * grow).astype(jnp.bfloat16)
        spread = jnp.exp(jnp.where(causal, cum_col - cum_row, 0.0))
        weights = jnp.where(causal, dot(query_n, key_n, (1, 1)) * spread, 0.0).astype(jnp.bfloat16)
        key_decay = (key_f * jnp.exp(last - cum_col)).astype(jnp.bfloat16)
        erase = dot(key_mix, key_decay, (0, 0)).astype(jnp.bfloat16)
        write = dot(new_base.astype(jnp.bfloat16), key_decay, (0, 0))
        held = state.astype(jnp.bfloat16)
        fresh = (new_base - dot(key_mix, held, (1, 1))).astype(jnp.bfloat16)
        out_ref[span, :] = (dot(query_gate, held, (1, 1)) + dot(weights, fresh, (1, 0))).astype(
            jnp.bfloat16
        )
        state = jnp.exp(last) * state + (write - dot(held, erase, (1, 0)))
    state_ref[...] = state


def delta_rule(queries, key_rows, values, inverse, gates, rate):
    seq_len, key_dim = queries.shape
    value_dim = values.shape[1]
    block_size = inverse.shape[1]
    block_count = seq_len // block_size
    chunk = 8 * block_size

    def rows(width):
        return pl.BlockSpec((chunk, width), lambda i: (i, 0))

    return pl.pallas_call(
        functools.partial(delta_kernel, block_size),
        grid=(seq_len // chunk,),
        out_shape=jax.ShapeDtypeStruct((seq_len, value_dim), jnp.bfloat16),
        in_specs=[
            rows(key_dim),
            rows(key_dim),
            rows(value_dim),
            rows(block_size),
            pl.BlockSpec((2, block_count, block_size), lambda i: (0, 0, 0)),
            pl.BlockSpec((1, 1), lambda i: (0, 0), memory_space=pltpu.SMEM),
        ],
        out_specs=rows(value_dim),
        scratch_shapes=[
            pltpu.VMEM((value_dim, key_dim), jnp.float32),
            pltpu.VMEM((block_count, block_size), jnp.float32),
            pltpu.VMEM((block_count, block_size), jnp.float32),
        ],
        name="delta_rule",
    )(queries, key_rows, values, inverse, gates, rate)


def per_device(
    hidden_in,
    route_ids,
    route_gates,
    language,
    allowed,
    w_gate,
    w_up,
    w_down,
    gate_proj,
    head_decay,
    query_in,
    key_in,
    value_in,
    block_inverse,
):
    exp_size = lax.axis_size("exp")
    seq_size = lax.axis_size("seq")
    tokens = hidden_in[0]
    tok_rows, model_width = tokens.shape
    routes_tok = route_ids.shape[2]
    experts = exp_size * w_gate.shape[0]
    capacity = 2 * tok_rows * routes_tok // experts
    flat_routes = route_ids[0].reshape(-1)
    expert_range = jnp.arange(experts, dtype=jnp.int32)
    onehot = (flat_routes[:, None] == expert_range[None, :]).astype(jnp.int32)
    earlier = jnp.cumsum(onehot, axis=0) - onehot
    slot_index = jnp.sum(earlier * onehot, axis=1)
    target = flat_routes * capacity + slot_index
    route_token = jnp.arange(tok_rows * routes_tok, dtype=jnp.int32) // routes_tok
    source_row = jnp.full((experts * capacity,), tok_rows, jnp.int32).at[target].set(route_token)
    padded = jnp.concatenate([tokens, jnp.zeros((1, model_width), tokens.dtype)], axis=0)
    outgoing = jnp.take(padded, source_row, axis=0).reshape(experts, capacity, model_width)
    incoming = lax.all_to_all(outgoing, "exp", split_axis=0, concat_axis=0, tiled=True)
    expert_rows = incoming.reshape(-1, model_width)

    def add_rows(portion):
        return jnp.dot(expert_rows, portion, preferred_element_type=jnp.float32)

    gate_proj_h = add_rows(lax.all_gather(w_gate[0], "seq", axis=0, tiled=True))
    up_proj_h = add_rows(lax.all_gather(w_up[0], "seq", axis=0, tiled=True))
    hidden = (jax.nn.silu(gate_proj_h) * up_proj_h).astype(jnp.bfloat16)
    produced = jnp.dot(
        hidden,
        lax.all_gather(w_down[0], "seq", axis=0, tiled=True),
        preferred_element_type=jnp.float32,
    )
    produced = produced.astype(jnp.bfloat16).reshape(exp_size, -1, model_width)
    returned = lax.all_to_all(produced, "exp", split_axis=0, concat_axis=0, tiled=True)
    back_rows = jnp.take(returned.reshape(-1, model_width), target, axis=0).reshape(
        tok_rows, routes_tok, model_width
    )
    lang_count = allowed.shape[0]
    lang_table = jnp.any(allowed[:, :, None] == expert_range[None, None, :], axis=1).astype(
        jnp.float32
    )
    lang_hot = (language[0][:, None] == jnp.arange(lang_count, dtype=jnp.int32)[None, :]).astype(
        jnp.float32
    )
    token_allow = jnp.dot(lang_hot, lang_table, precision=highest)
    route_allow = jnp.sum(
        token_allow[:, None, :] * onehot.reshape(tok_rows, routes_tok, experts).astype(jnp.float32),
        axis=2,
    )
    route_weight = route_gates[0] * route_allow
    mixed = jnp.sum(route_weight[..., None] * back_rows.astype(jnp.float32), axis=1)
    routed = mixed.astype(jnp.bfloat16)
    residual = (tokens.astype(jnp.float32) + routed.astype(jnp.float32)).astype(jnp.bfloat16)
    logits = jnp.dot(residual, gate_proj, preferred_element_type=jnp.float32).astype(jnp.bfloat16)
    heads_v = head_decay.shape[0]
    heads_k = heads_v // 2
    key_dim = query_in.shape[2] // heads_k
    heads_dev = heads_v // seq_size
    beta_logit = logits[:, :heads_v]
    decay_logit = logits[:, heads_v:]
    queries = query_in[0]
    key_rows = key_in[0]
    values_in = value_in[0]
    inverse_in = block_inverse[0]

    def repeated(values):
        return jnp.repeat(values.reshape(tok_rows, heads_k, key_dim), 2, axis=1).reshape(
            tok_rows, -1
        )

    full_q, full_k, got_v, got_inv, got_beta, got_decay = (
        lax.all_to_all(repeated(queries), "seq", split_axis=1, concat_axis=0, tiled=True),
        lax.all_to_all(repeated(key_rows), "seq", split_axis=1, concat_axis=0, tiled=True),
        lax.all_to_all(values_in, "seq", split_axis=1, concat_axis=0, tiled=True),
        lax.all_to_all(inverse_in, "seq", split_axis=1, concat_axis=0, tiled=True),
        lax.all_to_all(beta_logit, "seq", split_axis=1, concat_axis=0, tiled=True),
        lax.all_to_all(decay_logit, "seq", split_axis=1, concat_axis=0, tiled=True),
    )
    seq_len = full_q.shape[0]
    block_size = inverse_in.shape[1] // heads_v
    block_count = seq_len // block_size
    head_start = lax.axis_index("seq") * heads_dev
    rate = lax.dynamic_slice_in_dim(head_decay, head_start, heads_dev).reshape(1, 1)
    gates = jnp.stack([got_beta, got_decay]).reshape(2, block_count, block_size)
    flat_out = delta_rule(full_q, full_k, got_v, got_inv, gates, rate)
    core_out = lax.all_to_all(flat_out, "seq", split_axis=0, concat_axis=1, tiled=True)
    return (routed[None], core_out[None])


def solution(mesh):
    in_specs = (
        P("exp", "seq", None),
        P("exp", "seq", None),
        P("exp", "seq", None),
        P("exp", "seq"),
        P(),
        P("exp", "seq", None),
        P("exp", "seq", None),
        P("exp", "seq", None),
        P(),
        P(),
        P("exp", "seq", None),
        P("exp", "seq", None),
        P("exp", "seq", None),
        P("exp", "seq", None),
    )
    out_specs = (P("exp", "seq", None), P("exp", "seq", None))
    return jax.shard_map(
        per_device, mesh=mesh, in_specs=in_specs, out_specs=out_specs, check_vma=False
    )
```

```python
import functools

import jax
import jax.numpy as jnp
from jax import lax
from jax.experimental import pallas as pl
from jax.experimental.pallas import tpu as pltpu
from jax.sharding import PartitionSpec as P

highest = lax.Precision.HIGHEST


def delta_kernel(block_size, q_ref, k_ref, v_ref, inv_ref, gate_ref, rate_ref, out_ref, state_ref, beta_ref, cum_ref):
    step = pl.program_id(0)
    chunk_rows, key_dim = q_ref.shape
    per_chunk = chunk_rows // block_size
    rows_i = lax.broadcasted_iota(jnp.int32, (block_size, block_size), 0)
    cols_i = lax.broadcasted_iota(jnp.int32, (block_size, block_size), 1)
    diagonal = rows_i == cols_i
    below = rows_i > cols_i
    causal = rows_i >= cols_i

    @pl.when(step == 0)
    def _():
        state_ref[...] = jnp.zeros_like(state_ref)
        beta_ref[...] = jax.nn.sigmoid(gate_ref[0].astype(jnp.float32))
        raw = gate_ref[1].astype(jnp.float32)
        soft = jnp.maximum(raw, 0.0) + jnp.log1p(jnp.exp(-jnp.abs(raw)))
        log_decay = -jnp.exp(rate_ref[0, 0]) * soft
        upper = (rows_i <= cols_i).astype(jnp.float32)
        cum_ref[...] = jnp.dot(
            log_decay, upper, precision=highest, preferred_element_type=jnp.float32
        )

    odd = lax.rem(lax.axis_index("seq"), 2) == 1

    def dot(a, b, contract):
        return lax.dot_general(
            a, b, ((contract[:1], contract[1:]), ((), ())), preferred_element_type=jnp.float32
        )

    def column(row):
        return jnp.sum(jnp.where(diagonal, row, 0.0), axis=1, keepdims=True)

    def normal(values, scale):
        vals = values.astype(jnp.float32)
        factor = lax.rsqrt(jnp.sum(vals * vals, axis=1, keepdims=True) + 1e-06) * scale
        return (vals * factor).astype(jnp.bfloat16)

    state = state_ref[...]
    for piece in range(per_chunk):
        span = pl.ds(piece * block_size, block_size)
        block = step * per_chunk + piece
        cum_row = cum_ref[pl.ds(block, 1), :]
        cum_col = column(cum_row)
        beta_col = column(beta_ref[pl.ds(block, 1), :])
        last = cum_row[:, block_size - 1 :]
        grow = jnp.exp(cum_col)
        query_n = normal(q_ref[span, :], key_dim ** (-0.5))
        key_n = normal(k_ref[span, :], 0.5)
        key_f = key_n.astype(jnp.float32)
        both = inv_ref[span, :].astype(jnp.float32)
        inverse = jnp.where(odd, both[:, block_size:], both[:, :block_size])
        solver = jnp.where(diagonal, 1.0, jnp.where(below, inverse, 0.0)).astype(jnp.bfloat16)
        beta_vals = (beta_col * v_ref[span, :].astype(jnp.float32)).astype(jnp.bfloat16)
        beta_keys = ((beta_col * grow) * key_f).astype(jnp.bfloat16)
        new_base = dot(solver, beta_vals, (1, 0))
        key_mix = dot(solver, beta_keys, (1, 0)).astype(jnp.bfloat16)
        query_gate = (query_n.astype(jnp.float32) * grow).astype(jnp.bfloat16)
        spread = jnp.exp(jnp.where(causal, cum_col - cum_row, 0.0))
        weights = jnp.where(causal, dot(query_n, key_n, (1, 1)) * spread, 0.0).astype(jnp.bfloat16)
        key_decay = (key_f * jnp.exp(last - cum_col)).astype(jnp.bfloat16)
        erase = dot(key_mix, key_decay, (0, 0)).astype(jnp.bfloat16)
        write = dot(new_base.astype(jnp.bfloat16), key_decay, (0, 0))
        held = state.astype(jnp.bfloat16)
        fresh = (new_base - dot(key_mix, held, (1, 1))).astype(jnp.bfloat16)
        out_ref[span, :] = (dot(query_gate, held, (1, 1)) + dot(weights, fresh, (1, 0))).astype(
            jnp.bfloat16
        )
        state = jnp.exp(last) * state + (write - dot(held, erase, (1, 0)))
    state_ref[...] = state


def delta_rule(queries, key_rows, values, inverse, gates, rate):
    seq_len, key_dim = queries.shape
    value_dim = values.shape[1]
    block_size = inverse.shape[1] // 2
    block_count = seq_len // block_size
    chunk = 8 * block_size

    def rows(width):
        return pl.BlockSpec((chunk, width), lambda i: (i, 0))

    return pl.pallas_call(
        functools.partial(delta_kernel, block_size),
        grid=(seq_len // chunk,),
        out_shape=jax.ShapeDtypeStruct((seq_len, value_dim), jnp.bfloat16),
        in_specs=[
            rows(key_dim),
            rows(key_dim),
            rows(value_dim),
            rows(2 * block_size),
            pl.BlockSpec((2, block_count, block_size), lambda i: (0, 0, 0)),
            pl.BlockSpec((1, 1), lambda i: (0, 0), memory_space=pltpu.SMEM),
        ],
        out_specs=rows(value_dim),
        scratch_shapes=[
            pltpu.VMEM((value_dim, key_dim), jnp.float32),
            pltpu.VMEM((block_count, block_size), jnp.float32),
            pltpu.VMEM((block_count, block_size), jnp.float32),
        ],
        name="delta_rule",
    )(queries, key_rows, values, inverse, gates, rate)


MESH = pl.DeviceIdType.MESH


def greet(exp_peers, seq_peers):
    exp_size, seq_size = lax.axis_size("exp"), lax.axis_size("seq")
    exp_me, seq_me = lax.axis_index("exp"), lax.axis_index("seq")
    barrier = pltpu.get_barrier_semaphore()

    @pl.loop(1, exp_size)
    def _(r):
        pl.semaphore_signal(
            barrier, inc=1, device_id=(seq_me, lax.rem(exp_me + r, exp_size)), device_id_type=MESH
        )

    for first, count, place in seq_peers:

        @pl.loop(first, first + count)
        def _(r):
            pl.semaphore_signal(barrier, inc=1, device_id=(place(r), exp_me), device_id_type=MESH)

    pl.semaphore_wait(barrier, exp_peers + sum(count for _, count, _ in seq_peers))


def along_exp(rows_ref, landed_ref, send_sem, recv_sem):
    exp_size = lax.axis_size("exp")
    exp_me, seq_me = lax.axis_index("exp"), lax.axis_index("seq")

    def block(r):
        other = lax.rem(exp_me + r, exp_size)
        return pltpu.make_async_remote_copy(
            src_ref=rows_ref.at[other],
            dst_ref=landed_ref.at[exp_me],
            send_sem=send_sem.at[r],
            recv_sem=recv_sem.at[r],
            device_id=(seq_me, other),
            device_id_type=MESH,
        )

    own = pltpu.make_async_copy(rows_ref.at[exp_me], landed_ref.at[exp_me], send_sem.at[0])
    return block, own


def dispatch_kernel(
    rows_ref, wg_ref, wu_ref, wd_ref, landed_ref, full_g, full_u, full_d,
    send_sem, recv_sem, own_sem, wsend, wrecv, psend, precv,
):
    exp_size, seq_size = lax.axis_size("exp"), lax.axis_size("seq")
    exp_me, seq_me = lax.axis_index("exp"), lax.axis_index("seq")
    chips = seq_size // 2
    chip, core = seq_me // 2, lax.rem(seq_me, 2)
    partner = chip * 2 + 1 - core

    def same_core(r):
        return lax.rem(chip + r, chips) * 2 + core

    greet(exp_size - 1, ((1, chips - 1, same_core), (0, 1, lambda r: partner)))
    block, own = along_exp(rows_ref, landed_ref, send_sem, recv_sem)
    pairs = ((wg_ref, full_g), (wu_ref, full_u), (wd_ref, full_d))

    def slot(full, shard, who):
        depth = shard.shape[0]
        return full.at[pl.ds(pl.multiple_of(who * depth, depth), depth)]

    def spread(i, r):
        shard, full = pairs[i]
        return pltpu.make_async_remote_copy(
            src_ref=shard,
            dst_ref=slot(full, shard, seq_me),
            send_sem=wsend.at[i, r],
            recv_sem=wrecv.at[i, r],
            device_id=(same_core(r), exp_me),
            device_id_type=MESH,
        )

    def relay(i, r):
        shard, full = pairs[i]
        origin = lax.rem(chip + chips - r, chips) * 2 + core
        return pltpu.make_async_remote_copy(
            src_ref=slot(full, shard, origin),
            dst_ref=slot(full, shard, origin),
            send_sem=psend.at[i, r],
            recv_sem=precv.at[i, r],
            device_id=(partner, exp_me),
            device_id_type=MESH,
        )

    def hand_over(i):
        shard, full = pairs[i]
        return pltpu.make_async_remote_copy(
            src_ref=shard,
            dst_ref=slot(full, shard, seq_me),
            send_sem=psend.at[i, 0],
            recv_sem=precv.at[i, 0],
            device_id=(partner, exp_me),
            device_id_type=MESH,
        )

    def keep(i):
        shard, full = pairs[i]
        return pltpu.make_async_copy(shard, slot(full, shard, seq_me), own_sem.at[i])

    @pl.loop(1, exp_size)
    def _(r):
        block(r).start()

    @pl.loop(1, chips)
    def _(r):
        for i in range(3):
            spread(i, r).start()

    for i in range(3):
        hand_over(i).start()
        keep(i).start()
    own.start()

    @pl.loop(1, chips)
    def _(r):
        for i in range(3):
            spread(i, r).wait_recv()
            relay(i, r).start()

    for i in range(3):
        keep(i).wait()
        hand_over(i).wait()

    @pl.loop(1, chips)
    def _(r):
        for i in range(3):
            spread(i, r).wait_send()
            relay(i, r).wait()

    own.wait()

    @pl.loop(1, exp_size)
    def _(r):
        block(r).wait()


def dispatch(rows, wg, wu, wd):
    exp_size, seq_size = lax.axis_size("exp"), lax.axis_size("seq")
    chips = seq_size // 2
    hbm = pl.BlockSpec(memory_space=pl.ANY)

    def full(shard):
        return jax.ShapeDtypeStruct((shard.shape[0] * seq_size, shard.shape[1]), shard.dtype)

    return pl.pallas_call(
        dispatch_kernel,
        out_shape=(jax.ShapeDtypeStruct(rows.shape, rows.dtype), full(wg), full(wu), full(wd)),
        in_specs=[hbm] * 4,
        out_specs=(hbm,) * 4,
        scratch_shapes=[
            pltpu.SemaphoreType.DMA((exp_size,)),
            pltpu.SemaphoreType.DMA((exp_size,)),
            pltpu.SemaphoreType.DMA((3,)),
        ]
        + [pltpu.SemaphoreType.DMA((3, chips))] * 4,
        compiler_params=pltpu.CompilerParams(collective_id=0, has_side_effects=True),
        name="dispatch",
    )(rows, wg, wu, wd)


def return_kernel(
    rows_ref, q_ref, k_ref, v_ref, inv_ref, landed_ref, full_q, full_k, full_v, full_inv,
    send_sem, recv_sem, own_sem, hsend, hrecv,
):
    exp_size, seq_size = lax.axis_size("exp"), lax.axis_size("seq")
    exp_me, seq_me = lax.axis_index("exp"), lax.axis_index("seq")
    greet(exp_size - 1, ((1, seq_size - 1, lambda r: lax.rem(seq_me + r, seq_size)),))
    block, own = along_exp(rows_ref, landed_ref, send_sem, recv_sem)
    pairs = ((q_ref, full_q, 2), (k_ref, full_k, 2), (v_ref, full_v, 1), (inv_ref, full_inv, 2))

    def ends(i, other):
        source, full, share = pairs[i]
        depth, width = source.shape[0], full.shape[1]
        return (
            source.at[:, pl.ds(pl.multiple_of((other // share) * width, width), width)],
            full.at[pl.ds(pl.multiple_of(seq_me * depth, depth), depth)],
        )

    def head(i, r):
        other = lax.rem(seq_me + r, seq_size)
        source, full = ends(i, other)
        return pltpu.make_async_remote_copy(
            src_ref=source,
            dst_ref=full,
            send_sem=hsend.at[i, r],
            recv_sem=hrecv.at[i, r],
            device_id=(other, exp_me),
            device_id_type=MESH,
        )

    def keep(i):
        source, full = ends(i, seq_me)
        return pltpu.make_async_copy(source, full, own_sem.at[i])

    @pl.loop(1, exp_size)
    def _(r):
        block(r).start()

    @pl.loop(1, seq_size)
    def _(r):
        for i in range(4):
            head(i, r).start()

    for i in range(4):
        keep(i).start()
    own.start()
    for i in range(4):
        keep(i).wait()
    own.wait()

    @pl.loop(1, seq_size)
    def _(r):
        for i in range(4):
            head(i, r).wait()

    @pl.loop(1, exp_size)
    def _(r):
        block(r).wait()


def give_back(rows, queries, key_rows, values, inverse, width):
    exp_size, seq_size = lax.axis_size("exp"), lax.axis_size("seq")
    hbm = pl.BlockSpec(memory_space=pl.ANY)
    landed = jax.ShapeDtypeStruct((seq_size * queries.shape[0], width), queries.dtype)
    return pl.pallas_call(
        return_kernel,
        out_shape=(jax.ShapeDtypeStruct(rows.shape, rows.dtype),) + (landed,) * 4,
        in_specs=[hbm] * 5,
        out_specs=(hbm,) * 5,
        scratch_shapes=[
            pltpu.SemaphoreType.DMA((exp_size,)),
            pltpu.SemaphoreType.DMA((exp_size,)),
            pltpu.SemaphoreType.DMA((4,)),
            pltpu.SemaphoreType.DMA((4, seq_size)),
            pltpu.SemaphoreType.DMA((4, seq_size)),
        ],
        compiler_params=pltpu.CompilerParams(collective_id=1, has_side_effects=True),
        name="give_back",
    )(rows, queries, key_rows, values, inverse)


def per_device(
    hidden_in,
    route_ids,
    route_gates,
    language,
    allowed,
    w_gate,
    w_up,
    w_down,
    gate_proj,
    head_decay,
    query_in,
    key_in,
    value_in,
    block_inverse,
):
    exp_size = lax.axis_size("exp")
    seq_size = lax.axis_size("seq")
    tokens = hidden_in[0]
    tok_rows, model_width = tokens.shape
    routes_tok = route_ids.shape[2]
    experts = exp_size * w_gate.shape[0]
    capacity = 2 * tok_rows * routes_tok // experts
    flat_routes = route_ids[0].reshape(-1)
    expert_range = jnp.arange(experts, dtype=jnp.int32)
    onehot = (flat_routes[:, None] == expert_range[None, :]).astype(jnp.int32)
    earlier = jnp.cumsum(onehot, axis=0) - onehot
    slot_index = jnp.sum(earlier * onehot, axis=1)
    target = flat_routes * capacity + slot_index
    route_token = jnp.arange(tok_rows * routes_tok, dtype=jnp.int32) // routes_tok
    source_row = jnp.full((experts * capacity,), tok_rows, jnp.int32).at[target].set(route_token)
    padded = jnp.concatenate([tokens, jnp.zeros((1, model_width), tokens.dtype)], axis=0)
    outgoing = jnp.take(padded, source_row, axis=0).reshape(experts, capacity, model_width)
    incoming, full_gate, full_up, full_down = dispatch(outgoing, w_gate[0], w_up[0], w_down[0])
    expert_rows = incoming.reshape(-1, model_width)
    gate_proj_h = jnp.dot(expert_rows, full_gate, preferred_element_type=jnp.float32)
    up_proj_h = jnp.dot(expert_rows, full_up, preferred_element_type=jnp.float32)
    hidden = (jax.nn.silu(gate_proj_h) * up_proj_h).astype(jnp.bfloat16)
    produced = jnp.dot(hidden, full_down, preferred_element_type=jnp.float32)
    produced = produced.astype(jnp.bfloat16).reshape(exp_size, -1, model_width)
    heads_v = head_decay.shape[0]
    heads_dev = heads_v // seq_size
    key_dim = 2 * query_in.shape[2] // heads_v
    returned, full_q, full_k, got_v, got_inv = give_back(
        produced, query_in[0], key_in[0], value_in[0], block_inverse[0], key_dim
    )
    back_rows = jnp.take(returned.reshape(-1, model_width), target, axis=0).reshape(
        tok_rows, routes_tok, model_width
    )
    lang_count = allowed.shape[0]
    lang_table = jnp.any(allowed[:, :, None] == expert_range[None, None, :], axis=1).astype(
        jnp.float32
    )
    lang_hot = (language[0][:, None] == jnp.arange(lang_count, dtype=jnp.int32)[None, :]).astype(
        jnp.float32
    )
    token_allow = jnp.dot(lang_hot, lang_table, precision=highest)
    route_allow = jnp.sum(
        token_allow[:, None, :] * onehot.reshape(tok_rows, routes_tok, experts).astype(jnp.float32),
        axis=2,
    )
    route_weight = route_gates[0] * route_allow
    mixed = jnp.sum(route_weight[..., None] * back_rows.astype(jnp.float32), axis=1)
    routed = mixed.astype(jnp.bfloat16)
    residual = (tokens.astype(jnp.float32) + routed.astype(jnp.float32)).astype(jnp.bfloat16)
    logits = jnp.dot(residual, gate_proj, preferred_element_type=jnp.float32).astype(jnp.bfloat16)
    seq_len = full_q.shape[0]
    block_size = block_inverse.shape[2] // heads_v
    block_count = seq_len // block_size
    leaving = logits.T.reshape(2, seq_size, tok_rows).transpose(1, 0, 2)
    gates = lax.all_to_all(leaving, "seq", split_axis=0, concat_axis=0, tiled=True)
    gates = gates.transpose(1, 0, 2).reshape(2, block_count, block_size)
    head_start = lax.axis_index("seq") * heads_dev
    rate = lax.dynamic_slice_in_dim(head_decay, head_start, heads_dev).reshape(1, 1)
    flat_out = delta_rule(full_q, full_k, got_v, got_inv, gates, rate)
    core_out = lax.all_to_all(flat_out, "seq", split_axis=0, concat_axis=1, tiled=True)
    return (routed[None], core_out[None])


def solution(mesh):
    in_specs = (
        P("exp", "seq", None),
        P("exp", "seq", None),
        P("exp", "seq", None),
        P("exp", "seq"),
        P(),
        P("exp", "seq", None),
        P("exp", "seq", None),
        P("exp", "seq", None),
        P(),
        P(),
        P("exp", "seq", None),
        P("exp", "seq", None),
        P("exp", "seq", None),
        P("exp", "seq", None),
    )
    out_specs = (P("exp", "seq", None), P("exp", "seq", None))
    return jax.shard_map(
        per_device, mesh=mesh, in_specs=in_specs, out_specs=out_specs, check_vma=False
    )
```

```python
import functools

import jax
import jax.numpy as jnp
from jax import lax
from jax.experimental import pallas as pl
from jax.experimental.pallas import tpu as pltpu
from jax.sharding import PartitionSpec as P

highest = lax.Precision.HIGHEST


def delta_kernel(block_size, q_ref, k_ref, v_ref, inv_ref, gate_ref, rate_ref, out_ref, state_ref, beta_ref, cum_ref):
    step = pl.program_id(0)
    chunk_rows, key_dim = q_ref.shape
    per_chunk = chunk_rows // block_size
    rows_i = lax.broadcasted_iota(jnp.int32, (block_size, block_size), 0)
    cols_i = lax.broadcasted_iota(jnp.int32, (block_size, block_size), 1)
    diagonal = rows_i == cols_i
    below = rows_i > cols_i
    causal = rows_i >= cols_i

    @pl.when(step == 0)
    def _():
        state_ref[...] = jnp.zeros_like(state_ref)
        beta_ref[...] = jax.nn.sigmoid(gate_ref[0].astype(jnp.float32))
        raw = gate_ref[1].astype(jnp.float32)
        soft = jnp.maximum(raw, 0.0) + jnp.log1p(jnp.exp(-jnp.abs(raw)))
        log_decay = -jnp.exp(rate_ref[0, 0]) * soft
        upper = (rows_i <= cols_i).astype(jnp.float32)
        cum_ref[...] = jnp.dot(
            log_decay, upper, precision=highest, preferred_element_type=jnp.float32
        )

    odd = lax.rem(lax.axis_index("seq"), 2) == 1

    def dot(a, b, contract):
        return lax.dot_general(
            a, b, ((contract[:1], contract[1:]), ((), ())), preferred_element_type=jnp.float32
        )

    def column(row):
        return jnp.sum(jnp.where(diagonal, row, 0.0), axis=1, keepdims=True)

    def normal(values, scale):
        vals = values.astype(jnp.float32)
        factor = lax.rsqrt(jnp.sum(vals * vals, axis=1, keepdims=True) + 1e-06) * scale
        return (vals * factor).astype(jnp.bfloat16)

    state = state_ref[...]
    for piece in range(per_chunk):
        span = pl.ds(piece * block_size, block_size)
        block = step * per_chunk + piece
        cum_row = cum_ref[pl.ds(block, 1), :]
        cum_col = column(cum_row)
        beta_col = column(beta_ref[pl.ds(block, 1), :])
        last = cum_row[:, block_size - 1 :]
        grow = jnp.exp(cum_col)
        query_n = normal(q_ref[span, :], key_dim ** (-0.5))
        key_n = normal(k_ref[span, :], 0.5)
        key_f = key_n.astype(jnp.float32)
        both = inv_ref[span, :].astype(jnp.float32)
        inverse = jnp.where(odd, both[:, block_size:], both[:, :block_size])
        solver = jnp.where(diagonal, 1.0, jnp.where(below, inverse, 0.0)).astype(jnp.bfloat16)
        beta_vals = (beta_col * v_ref[span, :].astype(jnp.float32)).astype(jnp.bfloat16)
        beta_keys = ((beta_col * grow) * key_f).astype(jnp.bfloat16)
        new_base = dot(solver, beta_vals, (1, 0))
        key_mix = dot(solver, beta_keys, (1, 0)).astype(jnp.bfloat16)
        query_gate = (query_n.astype(jnp.float32) * grow).astype(jnp.bfloat16)
        spread = jnp.exp(jnp.where(causal, cum_col - cum_row, 0.0))
        weights = jnp.where(causal, dot(query_n, key_n, (1, 1)) * spread, 0.0).astype(jnp.bfloat16)
        key_decay = (key_f * jnp.exp(last - cum_col)).astype(jnp.bfloat16)
        erase = dot(key_mix, key_decay, (0, 0)).astype(jnp.bfloat16)
        write = dot(new_base.astype(jnp.bfloat16), key_decay, (0, 0))
        held = state.astype(jnp.bfloat16)
        fresh = (new_base - dot(key_mix, held, (1, 1))).astype(jnp.bfloat16)
        out_ref[span, :] = (dot(query_gate, held, (1, 1)) + dot(weights, fresh, (1, 0))).astype(
            jnp.bfloat16
        )
        state = jnp.exp(last) * state + (write - dot(held, erase, (1, 0)))
    state_ref[...] = state


def delta_rule(queries, key_rows, values, inverse, gates, rate):
    seq_len, key_dim = queries.shape
    value_dim = values.shape[1]
    block_size = inverse.shape[1] // 2
    block_count = seq_len // block_size
    chunk = 8 * block_size

    def rows(width):
        return pl.BlockSpec((chunk, width), lambda i: (i, 0))

    return pl.pallas_call(
        functools.partial(delta_kernel, block_size),
        grid=(seq_len // chunk,),
        out_shape=jax.ShapeDtypeStruct((seq_len, value_dim), jnp.bfloat16),
        in_specs=[
            rows(key_dim),
            rows(key_dim),
            rows(value_dim),
            rows(2 * block_size),
            pl.BlockSpec((2, block_count, block_size), lambda i: (0, 0, 0)),
            pl.BlockSpec((1, 1), lambda i: (0, 0), memory_space=pltpu.SMEM),
        ],
        out_specs=rows(value_dim),
        scratch_shapes=[
            pltpu.VMEM((value_dim, key_dim), jnp.float32),
            pltpu.VMEM((block_count, block_size), jnp.float32),
            pltpu.VMEM((block_count, block_size), jnp.float32),
        ],
        name="delta_rule",
    )(queries, key_rows, values, inverse, gates, rate)


MESH = pl.DeviceIdType.MESH


def greet(exp_peers, seq_peers):
    exp_size, seq_size = lax.axis_size("exp"), lax.axis_size("seq")
    exp_me, seq_me = lax.axis_index("exp"), lax.axis_index("seq")
    barrier = pltpu.get_barrier_semaphore()

    @pl.loop(1, exp_size)
    def _(r):
        pl.semaphore_signal(
            barrier, inc=1, device_id=(seq_me, lax.rem(exp_me + r, exp_size)), device_id_type=MESH
        )

    for first, count, place in seq_peers:

        @pl.loop(first, first + count)
        def _(r):
            pl.semaphore_signal(barrier, inc=1, device_id=(place(r), exp_me), device_id_type=MESH)

    pl.semaphore_wait(barrier, exp_peers + sum(count for _, count, _ in seq_peers))


def plane(number):
    exp_size, reach = lax.axis_size("exp"), lax.axis_size("exp") // 2
    return lax.rem(
        lax.axis_index("exp") + exp_size + lax.rem(number, reach) - reach // 2, exp_size
    )


def plane_back(number):
    exp_size, reach = lax.axis_size("exp"), lax.axis_size("exp") // 2
    return lax.rem(
        lax.axis_index("exp") + exp_size - lax.rem(number, reach) + reach // 2, exp_size
    )


def along_exp(rows_ref, landed_ref, send_sem, recv_sem, own_sem, where):
    exp_size = lax.axis_size("exp")
    reach = exp_size // 2
    exp_me, seq_me = lax.axis_index("exp"), lax.axis_index("seq")

    def block(j):
        return pltpu.make_async_remote_copy(
            src_ref=rows_ref.at[j],
            dst_ref=landed_ref.at[j],
            send_sem=send_sem.at[j],
            recv_sem=recv_sem.at[j],
            device_id=(seq_me, where(j)),
            device_id_type=MESH,
        )

    def own(n):
        j = reach // 2 + n * reach
        return pltpu.make_async_copy(rows_ref.at[j], landed_ref.at[j], own_sem.at[n])

    def each(act, low, high):
        @pl.loop(low, high)
        def _(j):
            act(block(j))
            act(block(j + reach))

    def lower(act):
        each(act, 0, reach // 2)

    def upper(act):
        each(act, reach // 2 + 1, reach)

    return lower, upper, own


def dispatch_kernel(
    rows_ref, wg_ref, wu_ref, wd_ref,
    landed_ref, full_g, full_u, full_d, mid_g, mid_u, mid_d, far_g, far_u, far_d,
    send_sem, recv_sem, own_sem, keep_sem, csend, crecv, wsend, wrecv, psend, precv,
):
    exp_size, seq_size = lax.axis_size("exp"), lax.axis_size("seq")
    exp_me, seq_me = lax.axis_index("exp"), lax.axis_index("seq")
    chips = seq_size // 2
    chip, core = seq_me // 2, lax.rem(seq_me, 2)
    partner = chip * 2 + 1 - core
    quarter = lax.rem(exp_me + exp_size // 4, exp_size)

    def same_core(r):
        return lax.rem(chip + r, chips) * 2 + core

    greet(exp_size - 1, ((1, chips - 1, same_core), (0, 1, lambda r: partner)))
    lower, upper, own = along_exp(rows_ref, landed_ref, send_sem, recv_sem, own_sem, plane)
    pairs = (
        (wg_ref, full_g, 0), (wu_ref, full_u, 0), (wd_ref, full_d, 0),
        (far_g, full_g, 1), (far_u, full_u, 1), (far_d, full_d, 1),
    )
    legs = (
        (wg_ref, mid_g), (wu_ref, mid_u), (wd_ref, mid_d),
        (mid_g, far_g), (mid_u, far_u), (mid_d, far_d),
    )

    def cross(i):
        return pltpu.make_async_remote_copy(
            src_ref=legs[i][0],
            dst_ref=legs[i][1],
            send_sem=csend.at[i],
            recv_sem=crecv.at[i],
            device_id=(seq_me, quarter),
            device_id_type=MESH,
        )

    def slot(i, who):
        shard, full, which = pairs[i]
        depth = shard.shape[0]
        return full.at[which, pl.ds(pl.multiple_of(who * depth, depth), depth)]

    def spread(i, r):
        return pltpu.make_async_remote_copy(
            src_ref=pairs[i][0],
            dst_ref=slot(i, seq_me),
            send_sem=wsend.at[i, r],
            recv_sem=wrecv.at[i, r],
            device_id=(same_core(r), exp_me),
            device_id_type=MESH,
        )

    def relay(i, r):
        origin = lax.rem(chip + chips - r, chips) * 2 + core
        return pltpu.make_async_remote_copy(
            src_ref=slot(i, origin),
            dst_ref=slot(i, origin),
            send_sem=psend.at[i, r],
            recv_sem=precv.at[i, r],
            device_id=(partner, exp_me),
            device_id_type=MESH,
        )

    def hand_over(i):
        return pltpu.make_async_remote_copy(
            src_ref=pairs[i][0],
            dst_ref=slot(i, seq_me),
            send_sem=psend.at[i, 0],
            recv_sem=precv.at[i, 0],
            device_id=(partner, exp_me),
            device_id_type=MESH,
        )

    def keep(i):
        return pltpu.make_async_copy(pairs[i][0], slot(i, seq_me), keep_sem.at[i])

    def send_out(first):
        @pl.loop(1, chips)
        def _(r):
            for i in range(first, first + 3):
                spread(i, r).start()

        for i in range(first, first + 3):
            hand_over(i).start()
            keep(i).start()

    for i in range(3):
        cross(i).start()
    send_out(0)
    lower(lambda copy: copy.start())
    own(0).start()
    own(1).start()
    for i in range(3):
        cross(i).wait_recv()
        cross(i + 3).start()
    for i in range(3):
        cross(i + 3).wait_recv()
    send_out(3)
    upper(lambda copy: copy.start())

    for first in (0, 3):

        @pl.loop(1, chips)
        def _(r):
            for i in range(first, first + 3):
                spread(i, r).wait_recv()
                relay(i, r).start()

    for i in range(6):
        cross(i).wait_send()
        keep(i).wait()
        hand_over(i).wait()

    @pl.loop(1, chips)
    def _(r):
        for i in range(6):
            spread(i, r).wait_send()
            relay(i, r).wait()

    own(0).wait()
    own(1).wait()
    lower(lambda copy: copy.wait())
    upper(lambda copy: copy.wait())


def dispatch(rows, wg, wu, wd):
    exp_size, seq_size = lax.axis_size("exp"), lax.axis_size("seq")
    chips = seq_size // 2
    hbm = pl.BlockSpec(memory_space=pl.ANY)

    def full(shard):
        return jax.ShapeDtypeStruct((2, shard.shape[0] * seq_size, shard.shape[1]), shard.dtype)

    def like(array):
        return jax.ShapeDtypeStruct(array.shape, array.dtype)

    return pl.pallas_call(
        dispatch_kernel,
        out_shape=(like(rows), full(wg), full(wu), full(wd)) + (like(wg), like(wu), like(wd)) * 2,
        in_specs=[hbm] * 4,
        out_specs=(hbm,) * 10,
        scratch_shapes=[
            pltpu.SemaphoreType.DMA((exp_size,)),
            pltpu.SemaphoreType.DMA((exp_size,)),
            pltpu.SemaphoreType.DMA((2,)),
            pltpu.SemaphoreType.DMA((6,)),
            pltpu.SemaphoreType.DMA((6,)),
            pltpu.SemaphoreType.DMA((6,)),
        ]
        + [pltpu.SemaphoreType.DMA((6, chips))] * 4,
        compiler_params=pltpu.CompilerParams(collective_id=0, has_side_effects=True),
        name="dispatch",
    )(rows, wg, wu, wd)[:4]


def return_kernel(
    rows_ref, q_ref, k_ref, v_ref, inv_ref, landed_ref, full_q, full_k, full_v, full_inv,
    send_sem, recv_sem, own_sem, keep_sem, vsend, vrecv, hsend, hrecv, psend, precv,
):
    exp_size, seq_size = lax.axis_size("exp"), lax.axis_size("seq")
    exp_me, seq_me = lax.axis_index("exp"), lax.axis_index("seq")
    chips = seq_size // 2
    chip, core = seq_me // 2, lax.rem(seq_me, 2)
    partner = chip * 2 + 1 - core
    greet(exp_size - 1, ((1, seq_size - 1, lambda r: lax.rem(seq_me + r, seq_size)),))
    lower, upper, own = along_exp(rows_ref, landed_ref, send_sem, recv_sem, own_sem, plane_back)
    shared = ((q_ref, full_q), (k_ref, full_k), (inv_ref, full_inv))

    def piece(source, full, number):
        width = full.shape[1]
        return source.at[:, pl.ds(pl.multiple_of(number * width, width), width)]

    def slot(source, full, who):
        depth = source.shape[0]
        return full.at[pl.ds(pl.multiple_of(who * depth, depth), depth)]

    def head(i, r):
        other = lax.rem(chip + r, chips)
        return pltpu.make_async_remote_copy(
            src_ref=piece(*shared[i], other),
            dst_ref=slot(*shared[i], seq_me),
            send_sem=hsend.at[i, r],
            recv_sem=hrecv.at[i, r],
            device_id=(other * 2 + core, exp_me),
            device_id_type=MESH,
        )

    def relay(i, r):
        origin = lax.rem(chip + chips - r, chips) * 2 + core
        return pltpu.make_async_remote_copy(
            src_ref=slot(*shared[i], origin),
            dst_ref=slot(*shared[i], origin),
            send_sem=psend.at[i, r],
            recv_sem=precv.at[i, r],
            device_id=(partner, exp_me),
            device_id_type=MESH,
        )

    def hand_over(i):
        return pltpu.make_async_remote_copy(
            src_ref=piece(*shared[i], chip),
            dst_ref=slot(*shared[i], seq_me),
            send_sem=psend.at[i, 0],
            recv_sem=precv.at[i, 0],
            device_id=(partner, exp_me),
            device_id_type=MESH,
        )

    def keep(i):
        return pltpu.make_async_copy(
            piece(*shared[i], chip), slot(*shared[i], seq_me), keep_sem.at[i]
        )

    def value(r):
        other = lax.rem(seq_me + r, seq_size)
        return pltpu.make_async_remote_copy(
            src_ref=piece(v_ref, full_v, other),
            dst_ref=slot(v_ref, full_v, seq_me),
            send_sem=vsend.at[r],
            recv_sem=vrecv.at[r],
            device_id=(other, exp_me),
            device_id_type=MESH,
        )

    keep_v = pltpu.make_async_copy(
        piece(v_ref, full_v, seq_me), slot(v_ref, full_v, seq_me), keep_sem.at[3]
    )
    lower(lambda copy: copy.start())
    upper(lambda copy: copy.start())

    @pl.loop(1, chips)
    def _(r):
        for i in range(3):
            head(i, r).start()

    @pl.loop(1, seq_size)
    def _(r):
        value(r).start()

    for i in range(3):
        hand_over(i).start()
        keep(i).start()
    keep_v.start()
    own(0).start()
    own(1).start()

    @pl.loop(1, chips)
    def _(r):
        for i in range(3):
            head(i, r).wait_recv()
            relay(i, r).start()

    for i in range(3):
        keep(i).wait()
        hand_over(i).wait()
    keep_v.wait()
    own(0).wait()
    own(1).wait()

    @pl.loop(1, chips)
    def _(r):
        for i in range(3):
            head(i, r).wait_send()
            relay(i, r).wait()

    @pl.loop(1, seq_size)
    def _(r):
        value(r).wait()

    lower(lambda copy: copy.wait())
    upper(lambda copy: copy.wait())


def give_back(rows, queries, key_rows, values, inverse, width):
    exp_size, seq_size = lax.axis_size("exp"), lax.axis_size("seq")
    chips = seq_size // 2
    hbm = pl.BlockSpec(memory_space=pl.ANY)
    landed = jax.ShapeDtypeStruct((seq_size * queries.shape[0], width), queries.dtype)
    return pl.pallas_call(
        return_kernel,
        out_shape=(jax.ShapeDtypeStruct(rows.shape, rows.dtype),) + (landed,) * 4,
        in_specs=[hbm] * 5,
        out_specs=(hbm,) * 5,
        scratch_shapes=[
            pltpu.SemaphoreType.DMA((exp_size,)),
            pltpu.SemaphoreType.DMA((exp_size,)),
            pltpu.SemaphoreType.DMA((2,)),
            pltpu.SemaphoreType.DMA((4,)),
            pltpu.SemaphoreType.DMA((seq_size,)),
            pltpu.SemaphoreType.DMA((seq_size,)),
        ]
        + [pltpu.SemaphoreType.DMA((3, chips))] * 4,
        compiler_params=pltpu.CompilerParams(collective_id=1, has_side_effects=True),
        name="give_back",
    )(rows, queries, key_rows, values, inverse)


def per_device(
    hidden_in,
    route_ids,
    route_gates,
    language,
    allowed,
    w_gate,
    w_up,
    w_down,
    gate_proj,
    head_decay,
    query_in,
    key_in,
    value_in,
    block_inverse,
):
    exp_size = lax.axis_size("exp")
    seq_size = lax.axis_size("seq")
    tokens = hidden_in[0]
    tok_rows, model_width = tokens.shape
    routes_tok = route_ids.shape[2]
    experts = exp_size * w_gate.shape[0]
    capacity = 2 * tok_rows * routes_tok // experts
    flat_routes = route_ids[0].reshape(-1)
    expert_range = jnp.arange(experts, dtype=jnp.int32)
    onehot = (flat_routes[:, None] == expert_range[None, :]).astype(jnp.int32)
    earlier = jnp.cumsum(onehot, axis=0) - onehot
    slot_index = jnp.sum(earlier * onehot, axis=1)
    turned = lax.rem(flat_routes - lax.axis_index("exp") + experts + experts // 4, experts)
    target = turned * capacity + slot_index
    route_token = jnp.arange(tok_rows * routes_tok, dtype=jnp.int32) // routes_tok
    source_row = jnp.full((experts * capacity,), tok_rows, jnp.int32).at[target].set(route_token)
    padded = jnp.concatenate([tokens, jnp.zeros((1, model_width), tokens.dtype)], axis=0)
    outgoing = jnp.take(padded, source_row, axis=0).reshape(experts, capacity, model_width)
    incoming, full_gate, full_up, full_down = dispatch(outgoing, w_gate[0], w_up[0], w_down[0])
    expert_rows = incoming.reshape(2, -1, model_width)
    produced = []
    for which in range(2):
        gate_proj_h = jnp.dot(
            expert_rows[which], full_gate[which], preferred_element_type=jnp.float32
        )
        up_proj_h = jnp.dot(expert_rows[which], full_up[which], preferred_element_type=jnp.float32)
        hidden = (jax.nn.silu(gate_proj_h) * up_proj_h).astype(jnp.bfloat16)
        produced.append(
            jnp.dot(hidden, full_down[which], preferred_element_type=jnp.float32).astype(
                jnp.bfloat16
            )
        )
    produced = jnp.concatenate(produced, axis=0).reshape(exp_size, -1, model_width)
    heads_v = head_decay.shape[0]
    heads_dev = heads_v // seq_size
    key_dim = 2 * query_in.shape[2] // heads_v
    returned, full_q, full_k, got_v, got_inv = give_back(
        produced, query_in[0], key_in[0], value_in[0], block_inverse[0], key_dim
    )
    back_rows = jnp.take(returned.reshape(-1, model_width), target, axis=0).reshape(
        tok_rows, routes_tok, model_width
    )
    lang_count = allowed.shape[0]
    lang_table = jnp.any(allowed[:, :, None] == expert_range[None, None, :], axis=1).astype(
        jnp.float32
    )
    lang_hot = (language[0][:, None] == jnp.arange(lang_count, dtype=jnp.int32)[None, :]).astype(
        jnp.float32
    )
    token_allow = jnp.dot(lang_hot, lang_table, precision=highest)
    route_allow = jnp.sum(
        token_allow[:, None, :] * onehot.reshape(tok_rows, routes_tok, experts).astype(jnp.float32),
        axis=2,
    )
    route_weight = route_gates[0] * route_allow
    mixed = jnp.sum(route_weight[..., None] * back_rows.astype(jnp.float32), axis=1)
    routed = mixed.astype(jnp.bfloat16)
    residual = (tokens.astype(jnp.float32) + routed.astype(jnp.float32)).astype(jnp.bfloat16)
    logits = jnp.dot(residual, gate_proj, preferred_element_type=jnp.float32).astype(jnp.bfloat16)
    seq_len = full_q.shape[0]
    block_size = block_inverse.shape[2] // heads_v
    block_count = seq_len // block_size
    leaving = logits.T.reshape(2, seq_size, tok_rows).transpose(1, 0, 2)
    gates = lax.all_to_all(leaving, "seq", split_axis=0, concat_axis=0, tiled=True)
    gates = gates.transpose(1, 0, 2).reshape(2, block_count, block_size)
    head_start = lax.axis_index("seq") * heads_dev
    rate = lax.dynamic_slice_in_dim(head_decay, head_start, heads_dev).reshape(1, 1)
    flat_out = delta_rule(full_q, full_k, got_v, got_inv, gates, rate)
    core_out = lax.all_to_all(flat_out, "seq", split_axis=0, concat_axis=1, tiled=True)
    return (routed[None], core_out[None])


def solution(mesh):
    in_specs = (
        P("exp", "seq", None),
        P("exp", "seq", None),
        P("exp", "seq", None),
        P("exp", "seq"),
        P(),
        P("exp", "seq", None),
        P("exp", "seq", None),
        P("exp", "seq", None),
        P(),
        P(),
        P("exp", "seq", None),
        P("exp", "seq", None),
        P("exp", "seq", None),
        P("exp", "seq", None),
    )
    out_specs = (P("exp", "seq", None), P("exp", "seq", None))
    return jax.shard_map(
        per_device, mesh=mesh, in_specs=in_specs, out_specs=out_specs, check_vma=False
    )
```

```python
import functools

import jax
import jax.numpy as jnp
from jax import lax
from jax.experimental import pallas as pl
from jax.experimental.pallas import tpu as pltpu
from jax.sharding import PartitionSpec as P

highest = lax.Precision.HIGHEST


def delta_kernel(
    block_size, q_ref, k_ref, v_ref, inv_ref, gate_ref, rate_ref, out_ref,
    state_ref, beta_ref, cum_ref, done_ref, gates_ref, gsend, grecv, osend, orecv,
):
    step = pl.program_id(0)
    chunk_rows, key_dim = q_ref.shape
    per_chunk = chunk_rows // block_size
    rows_i = lax.broadcasted_iota(jnp.int32, (block_size, block_size), 0)
    cols_i = lax.broadcasted_iota(jnp.int32, (block_size, block_size), 1)
    diagonal = rows_i == cols_i
    below = rows_i > cols_i
    causal = rows_i >= cols_i
    seq_size = lax.axis_size("seq")
    exp_me, seq_me = lax.axis_index("exp"), lax.axis_index("seq")
    tok_rows = out_ref.shape[0]
    owners = chunk_rows // tok_rows

    def gate_copy(r):
        other = lax.rem(seq_me + r, seq_size)
        return pltpu.make_async_remote_copy(
            src_ref=gate_ref.at[other],
            dst_ref=gates_ref.at[seq_me],
            send_sem=gsend.at[r],
            recv_sem=grecv.at[r],
            device_id=(other, exp_me),
            device_id_type=MESH,
        )

    def out_ends(owner):
        return (
            done_ref.at[pl.ds(pl.multiple_of(owner * tok_rows, tok_rows), tok_rows)],
            out_ref.at[:, pl.ds(pl.multiple_of(seq_me * key_dim, key_dim), key_dim)],
        )

    def out_copy(r):
        other = lax.rem(seq_me + r, seq_size)
        source, landing = out_ends(other)
        return pltpu.make_async_remote_copy(
            src_ref=source,
            dst_ref=landing,
            send_sem=osend.at[r],
            recv_sem=orecv.at[r],
            device_id=(other, exp_me),
            device_id_type=MESH,
        )

    def out_own():
        source, landing = out_ends(seq_me)
        return pltpu.make_async_copy(source, landing, osend.at[0])

    def send_chunk(number):
        for place in range(owners):
            owner = number * owners + place

            @pl.when(owner != seq_me)
            def _():
                out_copy(lax.rem(owner + seq_size - seq_me, seq_size)).start()

            @pl.when(owner == seq_me)
            def _():
                out_own().start()

    @pl.when(step == 0)
    def _():
        barrier = pltpu.get_barrier_semaphore()

        @pl.loop(1, seq_size)
        def _(r):
            pl.semaphore_signal(
                barrier,
                inc=1,
                device_id=(lax.rem(seq_me + r, seq_size), exp_me),
                device_id_type=MESH,
            )

        pl.semaphore_wait(barrier, seq_size - 1)
        own = pltpu.make_async_copy(gate_ref.at[seq_me], gates_ref.at[seq_me], gsend.at[0])
        own.start()

        @pl.loop(1, seq_size)
        def _(r):
            gate_copy(r).start()

        state_ref[...] = jnp.zeros_like(state_ref)
        own.wait()

        @pl.loop(1, seq_size)
        def _(r):
            gate_copy(r).wait()

        beta_ref[...] = jax.nn.sigmoid(gates_ref[:, 0, :])
        raw = gates_ref[:, 1, :]
        soft = jnp.maximum(raw, 0.0) + jnp.log1p(jnp.exp(-jnp.abs(raw)))
        log_decay = -jnp.exp(rate_ref[0, 0]) * soft
        rows_t = lax.broadcasted_iota(jnp.int32, (tok_rows, tok_rows), 0)
        cols_t = lax.broadcasted_iota(jnp.int32, (tok_rows, tok_rows), 1)
        same = rows_t // block_size == cols_t // block_size
        upper = jnp.where(same & (rows_t <= cols_t), 1.0, 0.0)
        cum_ref[...] = jnp.dot(
            log_decay, upper, precision=highest, preferred_element_type=jnp.float32
        )

    @pl.when(step > 0)
    def _():
        send_chunk(step - 1)

    odd = lax.rem(lax.axis_index("seq"), 2) == 1

    def dot(a, b, contract):
        return lax.dot_general(
            a, b, ((contract[:1], contract[1:]), ((), ())), preferred_element_type=jnp.float32
        )

    def column(row):
        return jnp.sum(jnp.where(diagonal, row, 0.0), axis=1, keepdims=True)

    def normal(values, scale):
        vals = values.astype(jnp.float32)
        factor = lax.rsqrt(jnp.sum(vals * vals, axis=1, keepdims=True) + 1e-06) * scale
        return (vals * factor).astype(jnp.bfloat16)

    state = state_ref[...]
    for piece in range(per_chunk):
        span = pl.ds(piece * block_size, block_size)
        fold = tok_rows // block_size
        line = pl.ds(step * owners + piece // fold, 1)
        part = slice(piece % fold * block_size, (piece % fold + 1) * block_size)
        cum_row = cum_ref[line, part]
        cum_col = column(cum_row)
        beta_col = column(beta_ref[line, part])
        last = cum_row[:, block_size - 1 :]
        grow = jnp.exp(cum_col)
        query_n = normal(q_ref[span, :], key_dim ** (-0.5))
        key_n = normal(k_ref[span, :], 0.5)
        key_f = key_n.astype(jnp.float32)
        both = inv_ref[span, :].astype(jnp.float32)
        inverse = jnp.where(odd, both[:, block_size:], both[:, :block_size])
        solver = jnp.where(diagonal, 1.0, jnp.where(below, inverse, 0.0)).astype(jnp.bfloat16)
        beta_vals = (beta_col * v_ref[span, :].astype(jnp.float32)).astype(jnp.bfloat16)
        beta_keys = ((beta_col * grow) * key_f).astype(jnp.bfloat16)
        new_base = dot(solver, beta_vals, (1, 0))
        key_mix = dot(solver, beta_keys, (1, 0)).astype(jnp.bfloat16)
        query_gate = (query_n.astype(jnp.float32) * grow).astype(jnp.bfloat16)
        spread = jnp.exp(jnp.where(causal, cum_col - cum_row, 0.0))
        weights = jnp.where(causal, dot(query_n, key_n, (1, 1)) * spread, 0.0).astype(jnp.bfloat16)
        key_decay = (key_f * jnp.exp(last - cum_col)).astype(jnp.bfloat16)
        erase = dot(key_mix, key_decay, (0, 0)).astype(jnp.bfloat16)
        write = dot(new_base.astype(jnp.bfloat16), key_decay, (0, 0))
        held = state.astype(jnp.bfloat16)
        fresh = (new_base - dot(key_mix, held, (1, 1))).astype(jnp.bfloat16)
        spot = pl.ds(pl.multiple_of(step * chunk_rows + piece * block_size, block_size), block_size)
        done_ref[spot, :] = (dot(query_gate, held, (1, 1)) + dot(weights, fresh, (1, 0))).astype(
            jnp.bfloat16
        )
        state = jnp.exp(last) * state + (write - dot(held, erase, (1, 0)))
    state_ref[...] = state

    @pl.when(step == pl.num_programs(0) - 1)
    def _():
        send_chunk(step)
        out_own().wait()

        @pl.loop(1, seq_size)
        def _(r):
            out_copy(r).wait()


def delta_rule(queries, key_rows, values, inverse, gates, rate):
    seq_len, key_dim = queries.shape
    value_dim = values.shape[1]
    block_size = inverse.shape[1] // 2
    seq_size = lax.axis_size("seq")
    tok_rows = seq_len // seq_size
    chunk = 4 * tok_rows

    def rows(width):
        return pl.BlockSpec((chunk, width), lambda i: (i, 0))

    return pl.pallas_call(
        functools.partial(delta_kernel, block_size),
        grid=(seq_len // chunk,),
        out_shape=jax.ShapeDtypeStruct((tok_rows, seq_size * value_dim), jnp.bfloat16),
        in_specs=[
            rows(key_dim),
            rows(key_dim),
            rows(value_dim),
            rows(2 * block_size),
            pl.BlockSpec(memory_space=pl.ANY),
            pl.BlockSpec((1, 1), lambda i: (0, 0), memory_space=pltpu.SMEM),
        ],
        out_specs=pl.BlockSpec(memory_space=pl.ANY),
        scratch_shapes=[
            pltpu.VMEM((value_dim, key_dim), jnp.float32),
            pltpu.VMEM((seq_size, tok_rows), jnp.float32),
            pltpu.VMEM((seq_size, tok_rows), jnp.float32),
            pltpu.VMEM((seq_len, value_dim), jnp.bfloat16),
            pltpu.VMEM(gates.shape, jnp.float32),
        ]
        + [pltpu.SemaphoreType.DMA((seq_size,))] * 4,
        compiler_params=pltpu.CompilerParams(collective_id=2, has_side_effects=True),
        name="delta_rule",
    )(queries, key_rows, values, inverse, gates, rate)


MESH = pl.DeviceIdType.MESH


def greet(exp_peers, seq_peers):
    exp_size, seq_size = lax.axis_size("exp"), lax.axis_size("seq")
    exp_me, seq_me = lax.axis_index("exp"), lax.axis_index("seq")
    barrier = pltpu.get_barrier_semaphore()

    @pl.loop(1, exp_size)
    def _(r):
        pl.semaphore_signal(
            barrier, inc=1, device_id=(seq_me, lax.rem(exp_me + r, exp_size)), device_id_type=MESH
        )

    for first, count, place in seq_peers:

        @pl.loop(first, first + count)
        def _(r):
            pl.semaphore_signal(barrier, inc=1, device_id=(place(r), exp_me), device_id_type=MESH)

    pl.semaphore_wait(barrier, exp_peers + sum(count for _, count, _ in seq_peers))


def along_exp(rows_ref, landed_ref, send_sem, recv_sem):
    exp_size = lax.axis_size("exp")
    exp_me, seq_me = lax.axis_index("exp"), lax.axis_index("seq")

    def block(r):
        other = lax.rem(exp_me + r, exp_size)
        return pltpu.make_async_remote_copy(
            src_ref=rows_ref.at[other],
            dst_ref=landed_ref.at[exp_me],
            send_sem=send_sem.at[r],
            recv_sem=recv_sem.at[r],
            device_id=(seq_me, other),
            device_id_type=MESH,
        )

    own = pltpu.make_async_copy(rows_ref.at[exp_me], landed_ref.at[exp_me], send_sem.at[0])
    return block, own


def dispatch_kernel(
    rows_ref, wg_ref, wu_ref, wd_ref, landed_ref, full_g, full_u, full_d,
    send_sem, recv_sem, own_sem, wsend, wrecv, psend, precv,
):
    exp_size, seq_size = lax.axis_size("exp"), lax.axis_size("seq")
    exp_me, seq_me = lax.axis_index("exp"), lax.axis_index("seq")
    chips = seq_size // 2
    chip, core = seq_me // 2, lax.rem(seq_me, 2)
    partner = chip * 2 + 1 - core

    def same_core(r):
        return lax.rem(chip + r, chips) * 2 + core

    greet(exp_size - 1, ((1, chips - 1, same_core), (0, 1, lambda r: partner)))
    block, own = along_exp(rows_ref, landed_ref, send_sem, recv_sem)
    pairs = ((wg_ref, full_g), (wu_ref, full_u), (wd_ref, full_d))

    def slot(full, shard, who):
        depth = shard.shape[0]
        return full.at[pl.ds(pl.multiple_of(who * depth, depth), depth)]

    def spread(i, r):
        shard, full = pairs[i]
        return pltpu.make_async_remote_copy(
            src_ref=shard,
            dst_ref=slot(full, shard, seq_me),
            send_sem=wsend.at[i, r],
            recv_sem=wrecv.at[i, r],
            device_id=(same_core(r), exp_me),
            device_id_type=MESH,
        )

    def relay(i, r):
        shard, full = pairs[i]
        origin = lax.rem(chip + chips - r, chips) * 2 + core
        return pltpu.make_async_remote_copy(
            src_ref=slot(full, shard, origin),
            dst_ref=slot(full, shard, origin),
            send_sem=psend.at[i, r],
            recv_sem=precv.at[i, r],
            device_id=(partner, exp_me),
            device_id_type=MESH,
        )

    def hand_over(i):
        shard, full = pairs[i]
        return pltpu.make_async_remote_copy(
            src_ref=shard,
            dst_ref=slot(full, shard, seq_me),
            send_sem=psend.at[i, 0],
            recv_sem=precv.at[i, 0],
            device_id=(partner, exp_me),
            device_id_type=MESH,
        )

    def keep(i):
        shard, full = pairs[i]
        return pltpu.make_async_copy(shard, slot(full, shard, seq_me), own_sem.at[i])

    @pl.loop(1, exp_size)
    def _(r):
        block(r).start()

    @pl.loop(1, chips)
    def _(r):
        for i in range(3):
            spread(i, r).start()

    for i in range(3):
        hand_over(i).start()
        keep(i).start()
    own.start()

    @pl.loop(1, chips)
    def _(r):
        for i in range(3):
            spread(i, r).wait_recv()
            relay(i, r).start()

    for i in range(3):
        keep(i).wait()
        hand_over(i).wait()

    @pl.loop(1, chips)
    def _(r):
        for i in range(3):
            spread(i, r).wait_send()
            relay(i, r).wait()

    own.wait()

    @pl.loop(1, exp_size)
    def _(r):
        block(r).wait()


def dispatch(rows, wg, wu, wd):
    exp_size, seq_size = lax.axis_size("exp"), lax.axis_size("seq")
    chips = seq_size // 2
    hbm = pl.BlockSpec(memory_space=pl.ANY)

    def full(shard):
        return jax.ShapeDtypeStruct((shard.shape[0] * seq_size, shard.shape[1]), shard.dtype)

    return pl.pallas_call(
        dispatch_kernel,
        out_shape=(jax.ShapeDtypeStruct(rows.shape, rows.dtype), full(wg), full(wu), full(wd)),
        in_specs=[hbm] * 4,
        out_specs=(hbm,) * 4,
        scratch_shapes=[
            pltpu.SemaphoreType.DMA((exp_size,)),
            pltpu.SemaphoreType.DMA((exp_size,)),
            pltpu.SemaphoreType.DMA((3,)),
        ]
        + [pltpu.SemaphoreType.DMA((3, chips))] * 4,
        compiler_params=pltpu.CompilerParams(collective_id=0, has_side_effects=True),
        name="dispatch",
    )(rows, wg, wu, wd)


def return_kernel(
    rows_ref, q_ref, k_ref, v_ref, inv_ref, landed_ref, full_q, full_k, full_v, full_inv,
    send_sem, recv_sem, own_sem, hsend, hrecv,
):
    exp_size, seq_size = lax.axis_size("exp"), lax.axis_size("seq")
    exp_me, seq_me = lax.axis_index("exp"), lax.axis_index("seq")
    greet(exp_size - 1, ((1, seq_size - 1, lambda r: lax.rem(seq_me + r, seq_size)),))
    block, own = along_exp(rows_ref, landed_ref, send_sem, recv_sem)
    pairs = ((q_ref, full_q, 2), (k_ref, full_k, 2), (v_ref, full_v, 1), (inv_ref, full_inv, 2))

    def ends(i, other):
        source, full, share = pairs[i]
        depth, width = source.shape[0], full.shape[1]
        return (
            source.at[:, pl.ds(pl.multiple_of((other // share) * width, width), width)],
            full.at[pl.ds(pl.multiple_of(seq_me * depth, depth), depth)],
        )

    def head(i, r):
        other = lax.rem(seq_me + r, seq_size)
        source, full = ends(i, other)
        return pltpu.make_async_remote_copy(
            src_ref=source,
            dst_ref=full,
            send_sem=hsend.at[i, r],
            recv_sem=hrecv.at[i, r],
            device_id=(other, exp_me),
            device_id_type=MESH,
        )

    def keep(i):
        source, full = ends(i, seq_me)
        return pltpu.make_async_copy(source, full, own_sem.at[i])

    @pl.loop(1, exp_size)
    def _(r):
        block(r).start()

    @pl.loop(1, seq_size)
    def _(r):
        for i in range(4):
            head(i, r).start()

    for i in range(4):
        keep(i).start()
    own.start()
    for i in range(4):
        keep(i).wait()
    own.wait()

    @pl.loop(1, seq_size)
    def _(r):
        for i in range(4):
            head(i, r).wait()

    @pl.loop(1, exp_size)
    def _(r):
        block(r).wait()


def give_back(rows, queries, key_rows, values, inverse, width):
    exp_size, seq_size = lax.axis_size("exp"), lax.axis_size("seq")
    hbm = pl.BlockSpec(memory_space=pl.ANY)
    landed = jax.ShapeDtypeStruct((seq_size * queries.shape[0], width), queries.dtype)
    return pl.pallas_call(
        return_kernel,
        out_shape=(jax.ShapeDtypeStruct(rows.shape, rows.dtype),) + (landed,) * 4,
        in_specs=[hbm] * 5,
        out_specs=(hbm,) * 5,
        scratch_shapes=[
            pltpu.SemaphoreType.DMA((exp_size,)),
            pltpu.SemaphoreType.DMA((exp_size,)),
            pltpu.SemaphoreType.DMA((4,)),
            pltpu.SemaphoreType.DMA((4, seq_size)),
            pltpu.SemaphoreType.DMA((4, seq_size)),
        ],
        compiler_params=pltpu.CompilerParams(collective_id=1, has_side_effects=True),
        name="give_back",
    )(rows, queries, key_rows, values, inverse)


def per_device(
    hidden_in,
    route_ids,
    route_gates,
    language,
    allowed,
    w_gate,
    w_up,
    w_down,
    gate_proj,
    head_decay,
    query_in,
    key_in,
    value_in,
    block_inverse,
):
    exp_size = lax.axis_size("exp")
    seq_size = lax.axis_size("seq")
    tokens = hidden_in[0]
    tok_rows, model_width = tokens.shape
    routes_tok = route_ids.shape[2]
    experts = exp_size * w_gate.shape[0]
    capacity = 2 * tok_rows * routes_tok // experts
    flat_routes = route_ids[0].reshape(-1)
    expert_range = jnp.arange(experts, dtype=jnp.int32)
    onehot = (flat_routes[:, None] == expert_range[None, :]).astype(jnp.int32)
    earlier = jnp.cumsum(onehot, axis=0) - onehot
    slot_index = jnp.sum(earlier * onehot, axis=1)
    target = flat_routes * capacity + slot_index
    route_token = jnp.arange(tok_rows * routes_tok, dtype=jnp.int32) // routes_tok
    source_row = jnp.full((experts * capacity,), tok_rows, jnp.int32).at[target].set(route_token)
    padded = jnp.concatenate([tokens, jnp.zeros((1, model_width), tokens.dtype)], axis=0)
    outgoing = jnp.take(padded, source_row, axis=0).reshape(experts, capacity, model_width)
    incoming, full_gate, full_up, full_down = dispatch(outgoing, w_gate[0], w_up[0], w_down[0])
    expert_rows = incoming.reshape(-1, model_width)
    gate_proj_h = jnp.dot(expert_rows, full_gate, preferred_element_type=jnp.float32)
    up_proj_h = jnp.dot(expert_rows, full_up, preferred_element_type=jnp.float32)
    hidden = (jax.nn.silu(gate_proj_h) * up_proj_h).astype(jnp.bfloat16)
    produced = jnp.dot(hidden, full_down, preferred_element_type=jnp.float32)
    produced = produced.astype(jnp.bfloat16).reshape(exp_size, -1, model_width)
    heads_v = head_decay.shape[0]
    heads_dev = heads_v // seq_size
    key_dim = 2 * query_in.shape[2] // heads_v
    returned, full_q, full_k, got_v, got_inv = give_back(
        produced, query_in[0], key_in[0], value_in[0], block_inverse[0], key_dim
    )
    back_rows = jnp.take(returned.reshape(-1, model_width), target, axis=0).reshape(
        tok_rows, routes_tok, model_width
    )
    lang_count = allowed.shape[0]
    lang_table = jnp.any(allowed[:, :, None] == expert_range[None, None, :], axis=1).astype(
        jnp.float32
    )
    lang_hot = (language[0][:, None] == jnp.arange(lang_count, dtype=jnp.int32)[None, :]).astype(
        jnp.float32
    )
    token_allow = jnp.dot(lang_hot, lang_table, precision=highest)
    route_allow = jnp.sum(
        token_allow[:, None, :] * onehot.reshape(tok_rows, routes_tok, experts).astype(jnp.float32),
        axis=2,
    )
    route_weight = route_gates[0] * route_allow
    mixed = jnp.sum(route_weight[..., None] * back_rows.astype(jnp.float32), axis=1)
    routed = mixed.astype(jnp.bfloat16)
    residual = (tokens.astype(jnp.float32) + routed.astype(jnp.float32)).astype(jnp.bfloat16)
    logits = jnp.dot(residual, gate_proj, preferred_element_type=jnp.float32).astype(jnp.bfloat16)
    leaving = logits.T.astype(jnp.float32).reshape(2, seq_size, tok_rows).transpose(1, 0, 2)
    gates = jnp.pad(leaving, ((0, 0), (0, 6), (0, 0)))
    head_start = lax.axis_index("seq") * heads_dev
    rate = lax.dynamic_slice_in_dim(head_decay, head_start, heads_dev).reshape(1, 1)
    core_out = delta_rule(full_q, full_k, got_v, got_inv, gates, rate)
    return (routed[None], core_out[None])


def solution(mesh):
    in_specs = (
        P("exp", "seq", None),
        P("exp", "seq", None),
        P("exp", "seq", None),
        P("exp", "seq"),
        P(),
        P("exp", "seq", None),
        P("exp", "seq", None),
        P("exp", "seq", None),
        P(),
        P(),
        P("exp", "seq", None),
        P("exp", "seq", None),
        P("exp", "seq", None),
        P("exp", "seq", None),
    )
    out_specs = (P("exp", "seq", None), P("exp", "seq", None))
    return jax.shard_map(
        per_device, mesh=mesh, in_specs=in_specs, out_specs=out_specs, check_vma=False
    )
```

```python
import functools

import jax
import jax.numpy as jnp
from jax import lax
from jax.experimental import pallas as pl
from jax.experimental.pallas import tpu as pltpu
from jax.sharding import PartitionSpec as P

highest = lax.Precision.HIGHEST


def delta_kernel(
    block_size, q_ref, k_ref, v_ref, inv_ref, gate_ref, rate_ref, out_ref,
    state_ref, beta_ref, cum_ref, done_ref, gates_ref, gsend, grecv, osend, orecv,
):
    step = pl.program_id(0)
    chunk_rows, key_dim = q_ref.shape
    per_chunk = chunk_rows // block_size
    rows_i = lax.broadcasted_iota(jnp.int32, (block_size, block_size), 0)
    cols_i = lax.broadcasted_iota(jnp.int32, (block_size, block_size), 1)
    diagonal = rows_i == cols_i
    below = rows_i > cols_i
    causal = rows_i >= cols_i
    seq_size = lax.axis_size("seq")
    exp_me, seq_me = lax.axis_index("exp"), lax.axis_index("seq")
    tok_rows = out_ref.shape[0]
    owners = chunk_rows // tok_rows

    def gate_copy(r):
        other = lax.rem(seq_me + r, seq_size)
        return pltpu.make_async_remote_copy(
            src_ref=gate_ref.at[other],
            dst_ref=gates_ref.at[seq_me],
            send_sem=gsend.at[r],
            recv_sem=grecv.at[r],
            device_id=(other, exp_me),
            device_id_type=MESH,
        )

    def out_ends(owner):
        return (
            done_ref.at[pl.ds(pl.multiple_of(owner * tok_rows, tok_rows), tok_rows)],
            out_ref.at[:, pl.ds(pl.multiple_of(seq_me * key_dim, key_dim), key_dim)],
        )

    def out_copy(r):
        other = lax.rem(seq_me + r, seq_size)
        source, landing = out_ends(other)
        return pltpu.make_async_remote_copy(
            src_ref=source,
            dst_ref=landing,
            send_sem=osend.at[r],
            recv_sem=orecv.at[r],
            device_id=(other, exp_me),
            device_id_type=MESH,
        )

    def out_own():
        source, landing = out_ends(seq_me)
        return pltpu.make_async_copy(source, landing, osend.at[0])

    def send_chunk(number):
        for place in range(owners):
            owner = number * owners + place

            @pl.when(owner != seq_me)
            def _():
                out_copy(lax.rem(owner + seq_size - seq_me, seq_size)).start()

            @pl.when(owner == seq_me)
            def _():
                out_own().start()

    @pl.when(step == 0)
    def _():
        barrier = pltpu.get_barrier_semaphore()

        @pl.loop(1, seq_size)
        def _(r):
            pl.semaphore_signal(
                barrier,
                inc=1,
                device_id=(lax.rem(seq_me + r, seq_size), exp_me),
                device_id_type=MESH,
            )

        pl.semaphore_wait(barrier, seq_size - 1)
        own = pltpu.make_async_copy(gate_ref.at[seq_me], gates_ref.at[seq_me], gsend.at[0])
        own.start()

        @pl.loop(1, seq_size)
        def _(r):
            gate_copy(r).start()

        state_ref[...] = jnp.zeros_like(state_ref)
        own.wait()

        @pl.loop(1, seq_size)
        def _(r):
            gate_copy(r).wait()

        beta_ref[...] = jax.nn.sigmoid(gates_ref[:, 0, :])
        raw = gates_ref[:, 1, :]
        soft = jnp.maximum(raw, 0.0) + jnp.log1p(jnp.exp(-jnp.abs(raw)))
        log_decay = -jnp.exp(rate_ref[0, 0]) * soft
        rows_t = lax.broadcasted_iota(jnp.int32, (tok_rows, tok_rows), 0)
        cols_t = lax.broadcasted_iota(jnp.int32, (tok_rows, tok_rows), 1)
        same = rows_t // block_size == cols_t // block_size
        upper = jnp.where(same & (rows_t <= cols_t), 1.0, 0.0)
        cum_ref[...] = jnp.dot(
            log_decay, upper, precision=highest, preferred_element_type=jnp.float32
        )

    @pl.when(step > 0)
    def _():
        send_chunk(step - 1)

    odd = lax.rem(lax.axis_index("seq"), 2) == 1

    def dot(a, b, contract):
        return lax.dot_general(
            a, b, ((contract[:1], contract[1:]), ((), ())), preferred_element_type=jnp.float32
        )

    def column(row):
        return jnp.sum(jnp.where(diagonal, row, 0.0), axis=1, keepdims=True)

    def normal(values, scale):
        vals = values.astype(jnp.float32)
        factor = lax.rsqrt(jnp.sum(vals * vals, axis=1, keepdims=True) + 1e-06) * scale
        return (vals * factor).astype(jnp.bfloat16)

    state = state_ref[...]
    for piece in range(per_chunk):
        span = pl.ds(piece * block_size, block_size)
        fold = tok_rows // block_size
        line = pl.ds(step * owners + piece // fold, 1)
        part = slice(piece % fold * block_size, (piece % fold + 1) * block_size)
        cum_row = cum_ref[line, part]
        cum_col = column(cum_row)
        beta_col = column(beta_ref[line, part])
        last = cum_row[:, block_size - 1 :]
        grow = jnp.exp(cum_col)
        query_n = normal(q_ref[span, :], key_dim ** (-0.5))
        key_n = normal(k_ref[span, :], 0.5)
        key_f = key_n.astype(jnp.float32)
        both = inv_ref[span, :].astype(jnp.float32)
        inverse = jnp.where(odd, both[:, block_size:], both[:, :block_size])
        solver = jnp.where(diagonal, 1.0, jnp.where(below, inverse, 0.0)).astype(jnp.bfloat16)
        beta_vals = (beta_col * v_ref[span, :].astype(jnp.float32)).astype(jnp.bfloat16)
        beta_keys = ((beta_col * grow) * key_f).astype(jnp.bfloat16)
        new_base = dot(solver, beta_vals, (1, 0))
        key_mix = dot(solver, beta_keys, (1, 0)).astype(jnp.bfloat16)
        query_gate = (query_n.astype(jnp.float32) * grow).astype(jnp.bfloat16)
        spread = jnp.exp(jnp.where(causal, cum_col - cum_row, 0.0))
        weights = jnp.where(causal, dot(query_n, key_n, (1, 1)) * spread, 0.0).astype(jnp.bfloat16)
        key_decay = (key_f * jnp.exp(last - cum_col)).astype(jnp.bfloat16)
        erase = dot(key_mix, key_decay, (0, 0)).astype(jnp.bfloat16)
        write = dot(new_base.astype(jnp.bfloat16), key_decay, (0, 0))
        held = state.astype(jnp.bfloat16)
        fresh = (new_base - dot(key_mix, held, (1, 1))).astype(jnp.bfloat16)
        spot = pl.ds(pl.multiple_of(step * chunk_rows + piece * block_size, block_size), block_size)
        done_ref[spot, :] = (dot(query_gate, held, (1, 1)) + dot(weights, fresh, (1, 0))).astype(
            jnp.bfloat16
        )
        state = jnp.exp(last) * state + (write - dot(held, erase, (1, 0)))
    state_ref[...] = state

    @pl.when(step == pl.num_programs(0) - 1)
    def _():
        send_chunk(step)
        out_own().wait()

        @pl.loop(1, seq_size)
        def _(r):
            out_copy(r).wait()


def delta_rule(queries, key_rows, values, inverse, gates, rate):
    seq_len, key_dim = queries.shape
    value_dim = values.shape[1]
    block_size = inverse.shape[1] // 2
    seq_size = lax.axis_size("seq")
    tok_rows = seq_len // seq_size
    chunk = 4 * tok_rows

    def rows(width):
        return pl.BlockSpec((chunk, width), lambda i: (i, 0))

    return pl.pallas_call(
        functools.partial(delta_kernel, block_size),
        grid=(seq_len // chunk,),
        out_shape=jax.ShapeDtypeStruct((tok_rows, seq_size * value_dim), jnp.bfloat16),
        in_specs=[
            rows(key_dim),
            rows(key_dim),
            rows(value_dim),
            rows(2 * block_size),
            pl.BlockSpec(memory_space=pl.ANY),
            pl.BlockSpec((1, 1), lambda i: (0, 0), memory_space=pltpu.SMEM),
        ],
        out_specs=pl.BlockSpec(memory_space=pl.ANY),
        scratch_shapes=[
            pltpu.VMEM((value_dim, key_dim), jnp.float32),
            pltpu.VMEM((seq_size, tok_rows), jnp.float32),
            pltpu.VMEM((seq_size, tok_rows), jnp.float32),
            pltpu.VMEM((seq_len, value_dim), jnp.bfloat16),
            pltpu.VMEM(gates.shape, jnp.float32),
        ]
        + [pltpu.SemaphoreType.DMA((seq_size,))] * 4,
        compiler_params=pltpu.CompilerParams(collective_id=2, has_side_effects=True),
        name="delta_rule",
    )(queries, key_rows, values, inverse, gates, rate)


MESH = pl.DeviceIdType.MESH


def greet(exp_peers, seq_peers):
    exp_size, seq_size = lax.axis_size("exp"), lax.axis_size("seq")
    exp_me, seq_me = lax.axis_index("exp"), lax.axis_index("seq")
    barrier = pltpu.get_barrier_semaphore()

    @pl.loop(1, exp_size)
    def _(r):
        pl.semaphore_signal(
            barrier, inc=1, device_id=(seq_me, lax.rem(exp_me + r, exp_size)), device_id_type=MESH
        )

    for first, count, place in seq_peers:

        @pl.loop(first, first + count)
        def _(r):
            pl.semaphore_signal(barrier, inc=1, device_id=(place(r), exp_me), device_id_type=MESH)

    pl.semaphore_wait(barrier, exp_peers + sum(count for _, count, _ in seq_peers))


def along_exp(rows_ref, landed_ref, send_sem, recv_sem):
    exp_size = lax.axis_size("exp")
    exp_me, seq_me = lax.axis_index("exp"), lax.axis_index("seq")

    def block(r):
        other = lax.rem(exp_me + r, exp_size)
        return pltpu.make_async_remote_copy(
            src_ref=rows_ref.at[other],
            dst_ref=landed_ref.at[exp_me],
            send_sem=send_sem.at[r],
            recv_sem=recv_sem.at[r],
            device_id=(seq_me, other),
            device_id_type=MESH,
        )

    own = pltpu.make_async_copy(rows_ref.at[exp_me], landed_ref.at[exp_me], send_sem.at[0])
    return block, own


def dispatch_kernel(
    rows_ref, wg_ref, wu_ref, wd_ref, landed_ref, full_g, full_u, full_d,
    send_sem, recv_sem, own_sem, wsend, wrecv, psend, precv,
):
    exp_size, seq_size = lax.axis_size("exp"), lax.axis_size("seq")
    exp_me, seq_me = lax.axis_index("exp"), lax.axis_index("seq")
    chips = seq_size // 2
    chip, core = seq_me // 2, lax.rem(seq_me, 2)
    partner = chip * 2 + 1 - core

    def same_core(r):
        return lax.rem(chip + r, chips) * 2 + core

    greet(exp_size - 1, ((1, chips - 1, same_core), (0, 1, lambda r: partner)))
    block, own = along_exp(rows_ref, landed_ref, send_sem, recv_sem)
    pairs = ((wg_ref, full_g), (wu_ref, full_u), (wd_ref, full_d))

    def slot(full, shard, who):
        depth = shard.shape[0]
        return full.at[pl.ds(pl.multiple_of(who * depth, depth), depth)]

    def spread(i, r):
        shard, full = pairs[i]
        return pltpu.make_async_remote_copy(
            src_ref=shard,
            dst_ref=slot(full, shard, seq_me),
            send_sem=wsend.at[i, r],
            recv_sem=wrecv.at[i, r],
            device_id=(same_core(r), exp_me),
            device_id_type=MESH,
        )

    def relay(i, r):
        shard, full = pairs[i]
        origin = lax.rem(chip + chips - r, chips) * 2 + core
        return pltpu.make_async_remote_copy(
            src_ref=slot(full, shard, origin),
            dst_ref=slot(full, shard, origin),
            send_sem=psend.at[i, r],
            recv_sem=precv.at[i, r],
            device_id=(partner, exp_me),
            device_id_type=MESH,
        )

    def hand_over(i):
        shard, full = pairs[i]
        return pltpu.make_async_remote_copy(
            src_ref=shard,
            dst_ref=slot(full, shard, seq_me),
            send_sem=psend.at[i, 0],
            recv_sem=precv.at[i, 0],
            device_id=(partner, exp_me),
            device_id_type=MESH,
        )

    def keep(i):
        shard, full = pairs[i]
        return pltpu.make_async_copy(shard, slot(full, shard, seq_me), own_sem.at[i])

    @pl.loop(1, chips)
    def _(r):
        for i in range(3):
            spread(i, r).start()

    @pl.loop(1, exp_size)
    def _(r):
        block(r).start()

    for i in range(3):
        hand_over(i).start()
        keep(i).start()
    own.start()

    @pl.loop(1, chips)
    def _(r):
        for i in range(3):
            spread(i, r).wait_recv()
            relay(i, r).start()

    for i in range(3):
        keep(i).wait()
        hand_over(i).wait()

    @pl.loop(1, chips)
    def _(r):
        for i in range(3):
            spread(i, r).wait_send()
            relay(i, r).wait()

    own.wait()

    @pl.loop(1, exp_size)
    def _(r):
        block(r).wait()


def dispatch(rows, wg, wu, wd):
    exp_size, seq_size = lax.axis_size("exp"), lax.axis_size("seq")
    chips = seq_size // 2
    hbm = pl.BlockSpec(memory_space=pl.ANY)

    def full(shard):
        return jax.ShapeDtypeStruct((shard.shape[0] * seq_size, shard.shape[1]), shard.dtype)

    return pl.pallas_call(
        dispatch_kernel,
        out_shape=(jax.ShapeDtypeStruct(rows.shape, rows.dtype), full(wg), full(wu), full(wd)),
        in_specs=[hbm] * 4,
        out_specs=(hbm,) * 4,
        scratch_shapes=[
            pltpu.SemaphoreType.DMA((exp_size,)),
            pltpu.SemaphoreType.DMA((exp_size,)),
            pltpu.SemaphoreType.DMA((3,)),
        ]
        + [pltpu.SemaphoreType.DMA((3, chips))] * 4,
        compiler_params=pltpu.CompilerParams(collective_id=0, has_side_effects=True),
        name="dispatch",
    )(rows, wg, wu, wd)


def return_kernel(
    rows_ref, q_ref, k_ref, v_ref, inv_ref, landed_ref, full_q, full_k, full_v, full_inv,
    send_sem, recv_sem, own_sem, hsend, hrecv,
):
    exp_size, seq_size = lax.axis_size("exp"), lax.axis_size("seq")
    exp_me, seq_me = lax.axis_index("exp"), lax.axis_index("seq")
    greet(exp_size - 1, ((1, seq_size - 1, lambda r: lax.rem(seq_me + r, seq_size)),))
    block, own = along_exp(rows_ref, landed_ref, send_sem, recv_sem)
    pairs = ((q_ref, full_q, 2), (k_ref, full_k, 2), (v_ref, full_v, 1), (inv_ref, full_inv, 2))

    def ends(i, other):
        source, full, share = pairs[i]
        depth, width = source.shape[0], full.shape[1]
        return (
            source.at[:, pl.ds(pl.multiple_of((other // share) * width, width), width)],
            full.at[pl.ds(pl.multiple_of(seq_me * depth, depth), depth)],
        )

    def head(i, r):
        other = lax.rem(seq_me + r, seq_size)
        source, full = ends(i, other)
        return pltpu.make_async_remote_copy(
            src_ref=source,
            dst_ref=full,
            send_sem=hsend.at[i, r],
            recv_sem=hrecv.at[i, r],
            device_id=(other, exp_me),
            device_id_type=MESH,
        )

    def keep(i):
        source, full = ends(i, seq_me)
        return pltpu.make_async_copy(source, full, own_sem.at[i])

    @pl.loop(1, exp_size)
    def _(r):
        block(r).start()

    @pl.loop(1, seq_size)
    def _(r):
        for i in range(4):
            head(i, r).start()

    for i in range(4):
        keep(i).start()
    own.start()
    for i in range(4):
        keep(i).wait()
    own.wait()

    @pl.loop(1, seq_size)
    def _(r):
        for i in range(4):
            head(i, r).wait()

    @pl.loop(1, exp_size)
    def _(r):
        block(r).wait()


def give_back(rows, queries, key_rows, values, inverse, width):
    exp_size, seq_size = lax.axis_size("exp"), lax.axis_size("seq")
    hbm = pl.BlockSpec(memory_space=pl.ANY)
    landed = jax.ShapeDtypeStruct((seq_size * queries.shape[0], width), queries.dtype)
    return pl.pallas_call(
        return_kernel,
        out_shape=(jax.ShapeDtypeStruct(rows.shape, rows.dtype),) + (landed,) * 4,
        in_specs=[hbm] * 5,
        out_specs=(hbm,) * 5,
        scratch_shapes=[
            pltpu.SemaphoreType.DMA((exp_size,)),
            pltpu.SemaphoreType.DMA((exp_size,)),
            pltpu.SemaphoreType.DMA((4,)),
            pltpu.SemaphoreType.DMA((4, seq_size)),
            pltpu.SemaphoreType.DMA((4, seq_size)),
        ],
        compiler_params=pltpu.CompilerParams(collective_id=1, has_side_effects=True),
        name="give_back",
    )(rows, queries, key_rows, values, inverse)


def per_device(
    hidden_in,
    route_ids,
    route_gates,
    language,
    allowed,
    w_gate,
    w_up,
    w_down,
    gate_proj,
    head_decay,
    query_in,
    key_in,
    value_in,
    block_inverse,
):
    exp_size = lax.axis_size("exp")
    seq_size = lax.axis_size("seq")
    tokens = hidden_in[0]
    tok_rows, model_width = tokens.shape
    routes_tok = route_ids.shape[2]
    experts = exp_size * w_gate.shape[0]
    capacity = 2 * tok_rows * routes_tok // experts
    flat_routes = route_ids[0].reshape(-1)
    expert_range = jnp.arange(experts, dtype=jnp.int32)
    onehot = (flat_routes[:, None] == expert_range[None, :]).astype(jnp.int32)
    earlier = jnp.cumsum(onehot, axis=0) - onehot
    slot_index = jnp.sum(earlier * onehot, axis=1)
    target = flat_routes * capacity + slot_index
    route_token = jnp.arange(tok_rows * routes_tok, dtype=jnp.int32) // routes_tok
    source_row = jnp.full((experts * capacity,), tok_rows, jnp.int32).at[target].set(route_token)
    padded = jnp.concatenate([tokens, jnp.zeros((1, model_width), tokens.dtype)], axis=0)
    outgoing = jnp.take(padded, source_row, axis=0).reshape(experts, capacity, model_width)
    incoming, full_gate, full_up, full_down = dispatch(outgoing, w_gate[0], w_up[0], w_down[0])
    expert_rows = incoming.reshape(-1, model_width)
    gate_proj_h = jnp.dot(expert_rows, full_gate, preferred_element_type=jnp.float32)
    up_proj_h = jnp.dot(expert_rows, full_up, preferred_element_type=jnp.float32)
    hidden = (jax.nn.silu(gate_proj_h) * up_proj_h).astype(jnp.bfloat16)
    produced = jnp.dot(hidden, full_down, preferred_element_type=jnp.float32)
    produced = produced.astype(jnp.bfloat16).reshape(exp_size, -1, model_width)
    heads_v = head_decay.shape[0]
    heads_dev = heads_v // seq_size
    key_dim = 2 * query_in.shape[2] // heads_v
    returned, full_q, full_k, got_v, got_inv = give_back(
        produced, query_in[0], key_in[0], value_in[0], block_inverse[0], key_dim
    )
    back_rows = jnp.take(returned.reshape(-1, model_width), target, axis=0).reshape(
        tok_rows, routes_tok, model_width
    )
    lang_count = allowed.shape[0]
    lang_table = jnp.any(allowed[:, :, None] == expert_range[None, None, :], axis=1).astype(
        jnp.float32
    )
    lang_hot = (language[0][:, None] == jnp.arange(lang_count, dtype=jnp.int32)[None, :]).astype(
        jnp.float32
    )
    token_allow = jnp.dot(lang_hot, lang_table, precision=highest)
    route_allow = jnp.sum(
        token_allow[:, None, :] * onehot.reshape(tok_rows, routes_tok, experts).astype(jnp.float32),
        axis=2,
    )
    route_weight = route_gates[0] * route_allow
    mixed = jnp.sum(route_weight[..., None] * back_rows.astype(jnp.float32), axis=1)
    routed = mixed.astype(jnp.bfloat16)
    residual = (tokens.astype(jnp.float32) + routed.astype(jnp.float32)).astype(jnp.bfloat16)
    logits = jnp.dot(residual, gate_proj, preferred_element_type=jnp.float32).astype(jnp.bfloat16)
    leaving = logits.T.astype(jnp.float32).reshape(2, seq_size, tok_rows).transpose(1, 0, 2)
    gates = jnp.pad(leaving, ((0, 0), (0, 6), (0, 0)))
    head_start = lax.axis_index("seq") * heads_dev
    rate = lax.dynamic_slice_in_dim(head_decay, head_start, heads_dev).reshape(1, 1)
    core_out = delta_rule(full_q, full_k, got_v, got_inv, gates, rate)
    return (routed[None], core_out[None])


def solution(mesh):
    in_specs = (
        P("exp", "seq", None),
        P("exp", "seq", None),
        P("exp", "seq", None),
        P("exp", "seq"),
        P(),
        P("exp", "seq", None),
        P("exp", "seq", None),
        P("exp", "seq", None),
        P(),
        P(),
        P("exp", "seq", None),
        P("exp", "seq", None),
        P("exp", "seq", None),
        P("exp", "seq", None),
    )
    out_specs = (P("exp", "seq", None), P("exp", "seq", None))
    return jax.shard_map(
        per_device, mesh=mesh, in_specs=in_specs, out_specs=out_specs, check_vma=False
    )
```
